32 devices in a mesh: seq: 8 (over z, core), fsdp: 4 (over y, x).
Axes of the slice: x: 2, y: 2, z: 4, core: 2. Of those that a mesh axis runs over, the one named last changes fastest.
Arguments:
- tokens: bfloat16 [1024, 8192], P('seq', 'fsdp'), may hold values from -6 to 6
- norm_gain: float32 [8192], replicated, may hold values from 0.25 to 1.75
- gate_proj: bfloat16 [8192, 8192], P('seq', 'fsdp'), may hold values from -0.0625 to 0.0625
- value_proj: bfloat16 [8192, 8192], P('seq', 'fsdp'), may hold values from -0.0625 to 0.0625
- step_proj: bfloat16 [8192, 128], P('seq', 'fsdp'), may hold values from -0.0625 to 0.0625
- state_proj: bfloat16 [8192, 4, 256], P('seq'), may hold values from -0.0625 to 0.0625
- conv_value: float32 [4, 8192], P(None, 'fsdp'), may hold values from -3 to 3
- conv_state: float32 [4, 4, 256], replicated, may hold values from -3 to 3
- step_bias: float32 [128], P('fsdp'), may hold values from -1 to 1
- decay_rate: float32 [128], P('fsdp'), may hold values from 0.00048828125 to 0.1
- skip_gain: float32 [128], P('fsdp'), may hold values from 0.5 to 1.5
- mix_gain: float32 [8192], P('fsdp'), may hold values from 0.25 to 1.75
- out_proj: bfloat16 [8192, 8192], P('fsdp', 'seq'), may hold values from -0.09375 to 0.09375
- doc_lengths: int32 [16], replicated, may hold values from 1 to 512, 1024 in all
Outputs:
- layer_out: bfloat16 [1024, 8192], P('seq', 'fsdp')
The draws below stay inside these ranges and needn't reach their ends.
Inputs may be any that keep to these rules, and one draw needn't show every extreme that they name: `doc_lengths`: the longest document has exactly 512 tokens, so it spans many stretches; the lengths sum to 1024.
All inputs are finite; a program needn't handle non-finite values.
Results may differ from the reference program's by a relative error of at most 0.014.
Values may be sent and summed in bfloat16 or wider, within the bound.
No kernel may reach another device: no remote copies, remote signals or barrier semaphores. Data moves between devices by JAX's collectives and lax.ppermute only.
A program may use at most 128 MiB of HBM per device.

```python
import math
import jax
import jax.numpy as jnp
import numpy as np
from jax import lax

D = 8192
H = 128
HEAD_DIM = 64
N = 128
G = 4
TOKENS = 1024
DOCS = 16


def spiked(entries, own_key, source, target, blocks, factor):
    def block_of(position):
        return (jnp.arange(entries.shape[position]) // (entries.shape[position] // blocks)).reshape((-1,) + (1,) * (entries.ndim - 1 - position))

    one_side = jax.random.permutation(own_key, blocks)[block_of(target)]
    far = (block_of(target) + blocks // 2) % blocks
    return jnp.where((block_of(source) == one_side) | (block_of(source) == far), factor * entries, entries)


def block_scale(own_key, extent, split, smallest, largest):
    factor_of = 1.0
    for axis_at, shards_of in split:
        heights = jax.random.uniform(jax.random.fold_in(jax.random.fold_in(own_key, 6), axis_at), (shards_of,), jnp.float32, smallest / len(split), largest / len(split))
        factor_of = factor_of * jnp.repeat(jnp.exp(heights), extent[axis_at] // shards_of).reshape((-1,) + (1,) * (len(extent) - 1 - axis_at))
    return factor_of


def length_profile(count, total, limit, skew):
    portions = [(1 << 20) // math.isqrt(standing ** skew) + 1 for standing in range(2, count + 1)]
    rest, holding = total - limit - (count - 1), [1] * (count - 1)
    while rest > 0:
        free = [i for i in range(count - 1) if holding[i] < limit]
        pool, left = sum([portions[i] for i in free]), rest
        for i in free:
            more = min(limit - holding[i], max(1, left * portions[i] // pool), rest)
            holding[i] = holding[i] + more
            rest = rest - more
    return np.array([limit] + holding)


def ragged_sizes(rng, amount, total, reach, skew):
    if amount == 2:
        one = jax.random.randint(rng, (), max(1, total - reach), min(reach, total - 1) + 1)
        return jnp.stack([one, total - one])
    lengths = jnp.asarray(length_profile(amount, total, reach, skew), jnp.int32)
    couples = (amount - 1) // 2
    source_of, sink = lengths[1:1 + 2 * couples:2], lengths[2:2 + 2 * couples:2]
    room = jnp.minimum(source_of - 1, reach - sink)
    moved = jax.random.randint(jax.random.fold_in(rng, 1), (couples,), 0, 1 << 20) % (room + 1)
    lengths = lengths.at[1:1 + 2 * couples:2].set(source_of - moved).at[2:2 + 2 * couples:2].set(sink + moved)
    return lengths[jax.random.permutation(jax.random.fold_in(rng, 2), amount)]


def scatter_about(key, dims, scale, bound, split=(), kind=jnp.bfloat16):
    level = block_scale(key, dims, split, -0.22, 0.18) if split else 1.0
    drawn = jax.random.normal(key, dims, jnp.float32) * scale * level
    return jnp.minimum(jnp.maximum(drawn, -bound), bound).astype(kind)


def gaussian_with(rng, extent, scale, bound, cuts, heavy, held_as=jnp.bfloat16):
    drawn = scale * jax.random.normal(rng, extent, jnp.float32)
    if cuts:
        drawn = drawn * block_scale(rng, extent, cuts, -0.22, 0.18)
    return jnp.clip(spiked(drawn, jax.random.fold_in(rng, 3), *heavy), -bound, bound).astype(held_as)


def setup_inputs(seed: int = 0) -> dict:
    key_list = jax.random.split(jax.random.key(seed), 15)
    return {
        "tokens": scatter_about(key_list[0], (TOKENS, D), 1.0, 6.0, ((0, 8), (1, 4))),
        "norm_gain": jnp.clip(1.0 + 0.15 * jax.random.normal(key_list[1], (D,), jnp.float32), 0.25, 1.75),
        "gate_proj": scatter_about(key_list[2], (D, H * HEAD_DIM), D ** -0.5, 0.0625, ((0, 8), (1, 4))),
        "value_proj": scatter_about(key_list[3], (D, H * HEAD_DIM), D ** -0.5, 0.0625, ((0, 8), (1, 4))),
        "step_proj": scatter_about(key_list[4], (D, H), D ** -0.5, 0.0625, ((0, 8), (1, 4))),
        "state_proj": scatter_about(key_list[5], (D, G, 2 * N), D ** -0.5, 0.0625, ((0, 8),)),
        "conv_value": scatter_about(key_list[6], (4, H * HEAD_DIM), 4 ** -0.5, 3.0, ((1, 4),), jnp.float32),
        "conv_state": scatter_about(key_list[7], (4, G, 2 * N), 4 ** -0.5, 3.0, (), jnp.float32),
        "step_bias": jnp.clip(jax.random.uniform(key_list[8], (H,), jnp.float32, -1.0, 1.0) * block_scale(key_list[8], (H,), ((0, 4),), -0.4, 0.0), -1.0, 1.0),
        "decay_rate": jnp.clip(jnp.exp(math.log(0.1) - 5.322034 * jax.random.uniform(key_list[9], (H,), jnp.float32) ** block_scale(key_list[9], (H,), ((0, 4),), -0.2, 0.2)), 0.00048828125, 0.1),
        "skip_gain": jnp.clip(0.5 + 1.0 * jax.random.uniform(key_list[10], (H,), jnp.float32) ** block_scale(key_list[10], (H,), ((0, 4),), -0.2, 0.2), 0.5, 1.5),
        "mix_gain": jnp.clip(1.0 + 0.15 * jax.random.normal(key_list[11], (H * HEAD_DIM,), jnp.float32), 0.25, 1.75),
        "out_proj": gaussian_with(key_list[12], (H * HEAD_DIM, D), (H * HEAD_DIM) ** -0.5, 0.09375, ((0, 4), (1, 8)), (0, 1, 8, 2.0)),
        "doc_lengths": ragged_sizes(key_list[13], DOCS, TOKENS, TOKENS // 2, 2).astype(jnp.int32),
    }


EPSILON = 1e-05
PRECISE = lax.Precision.HIGHEST

def reference(tokens, norm_gain, gate_proj, value_proj, step_proj, state_proj, conv_value, conv_state, step_bias, decay_rate, skip_gain, mix_gain, out_proj, doc_lengths):
    as_float = tokens.astype(jnp.float32)
    normed = (as_float * lax.rsqrt(lax.optimization_barrier(jnp.mean(as_float * as_float, axis=1, keepdims=True)) + EPSILON) * norm_gain).astype(jnp.bfloat16)
    gate = jnp.dot(normed, gate_proj, preferred_element_type=jnp.float32)
    raw_step = jnp.dot(normed, step_proj, preferred_element_type=jnp.float32)
    raw_values = jnp.dot(normed, value_proj, preferred_element_type=jnp.float32).astype(jnp.bfloat16)
    raw_states = jnp.dot(normed, state_proj.reshape(D, G * 2 * N), preferred_element_type=jnp.float32).astype(jnp.bfloat16).reshape(TOKENS, G, 2 * N)
    starts = (jnp.cumsum(doc_lengths) - doc_lengths).astype(jnp.int32)
    positions = jnp.arange(-3, TOKENS, dtype=jnp.int32)
    segment_ext = lax.optimization_barrier(jnp.sum(starts[None, :] <= positions[:, None], axis=1)).astype(jnp.int32) - 1
    segment = segment_ext[3:]
    padded_values = jnp.concatenate([jnp.zeros((3, H * HEAD_DIM), jnp.bfloat16), raw_values], axis=0)
    padded_states = jnp.concatenate([jnp.zeros((3, G, 2 * N), jnp.bfloat16), raw_states], axis=0)
    conv_values = jnp.zeros((TOKENS, H * HEAD_DIM), jnp.float32)
    conv_states = jnp.zeros((TOKENS, G, 2 * N), jnp.float32)
    for offset in range(4):
        same_doc = segment_ext[offset:offset + TOKENS] == segment
        conv_values = conv_values + jnp.where(same_doc[:, None], padded_values[offset:offset + TOKENS].astype(jnp.float32), 0.0) * conv_value[offset]
        conv_states = conv_states + jnp.where(same_doc[:, None, None], padded_states[offset:offset + TOKENS].astype(jnp.float32), 0.0) * conv_state[offset]
    rounded_values = lax.optimization_barrier(jax.nn.silu(conv_values).astype(jnp.bfloat16))
    rounded_states = lax.optimization_barrier(jax.nn.silu(conv_states).astype(jnp.bfloat16))
    inputs = rounded_values.astype(jnp.float32).reshape(TOKENS, H, HEAD_DIM)
    maps = rounded_states.astype(jnp.float32)
    in_map = maps[:, :, :N]
    out_map = maps[:, :, N:]
    step_size = jax.nn.softplus(raw_step + step_bias)
    log_decay = -decay_rate * step_size
    is_start = jnp.any(positions[3:, None] == starts[None, :], axis=1)
    per_group = H // G

    def advance(state, column):
        value_now, in_now, out_now, size_now, decay_now, start_now = column
        in_heads = jnp.repeat(in_now, per_group, axis=0)
        out_heads = jnp.repeat(out_now, per_group, axis=0)
        keep = jnp.where(start_now, 0.0, jnp.exp(decay_now))
        state = keep[:, None, None] * state + (size_now[:, None] * value_now)[:, :, None] * in_heads[:, None, :]
        return (state, jnp.einsum('hpn,hn->hp', state, out_heads, precision=PRECISE))
    initial = jnp.zeros((H, HEAD_DIM, N), jnp.float32)
    _, history = lax.scan(advance, initial, (inputs, in_map, out_map, step_size, log_decay, is_start))
    outputs = history + skip_gain[None, :, None] * inputs
    gated = outputs.reshape(TOKENS, H * HEAD_DIM) * jax.nn.silu(gate)
    grouped = gated.reshape(TOKENS, G, H * HEAD_DIM // G)
    mean_square = lax.optimization_barrier(jnp.mean(grouped * grouped, axis=2, keepdims=True))
    scaled = ((grouped * lax.rsqrt(mean_square + EPSILON)).reshape(TOKENS, H * HEAD_DIM) * mix_gain).astype(jnp.bfloat16)
    mixed = jnp.dot(scaled, out_proj, preferred_element_type=jnp.float32)
    return (as_float + mixed).astype(jnp.bfloat16)
```

```python
import jax
import jax.numpy as jnp
from jax import lax
from jax.experimental import pallas as pl
from jax.experimental.pallas import tpu as pltpu
from jax.sharding import PartitionSpec as P

H = 128
HEAD_DIM = 64
N = 128
G = 4


EPSILON = 1e-05
PRECISE = lax.Precision.HIGHEST


def from_behind(value, axis, steps):
    count = lax.axis_size(axis)
    leading, last = (max(0, -steps), min(count, count - steps))
    return lax.ppermute(value, axis, [(source, source + steps) for source in range(leading, last)])


def partner(block, axis, distance):
    count = lax.axis_size(axis)
    route = []
    for low in range(count):
        high = low | 1 << distance
        if high != low and high < count:
            route += [(low, high), (high, low)]
    return lax.ppermute(block, axis, route)


def by_stretch(
    tokens,
    norm_gain,
    gate_proj,
    value_proj,
    step_proj,
    state_proj,
    conv_value,
    conv_state,
    step_bias,
    decay_rate,
    skip_gain,
    mix_gain,
    out_proj,
    doc_lengths,
):
    span_rows = tokens.shape[0]
    seq_index = lax.axis_index("seq")
    fsdp_index = lax.axis_index("fsdp")
    head_count = step_bias.shape[0]
    inner_width = gate_proj.shape[1]
    group_devices = lax.axis_size("fsdp") // G
    group_index = fsdp_index // group_devices
    gathered = lax.all_gather(tokens, "fsdp", axis=1, tiled=True)
    as_float = gathered.astype(jnp.float32)
    normed = (
        as_float
        * lax.rsqrt(jnp.mean(as_float * as_float, axis=1, keepdims=True) + EPSILON)
        * norm_gain
    ).astype(jnp.bfloat16)
    state_cols = lax.dynamic_index_in_dim(state_proj, group_index, 1, keepdims=False)
    stacked = jnp.concatenate([gate_proj, value_proj, state_cols, step_proj], axis=1)
    spread = lax.all_to_all(normed, "seq", split_axis=1, concat_axis=0, tiled=True)
    summed = lax.psum_scatter(
        jnp.dot(spread, stacked, preferred_element_type=jnp.float32),
        "seq",
        scatter_dimension=0,
        tiled=True,
    )
    gate = summed[:, :inner_width]
    values = summed[:, inner_width : 2 * inner_width]
    states = summed[:, 2 * inner_width : 2 * inner_width + 2 * N]
    raw_step = summed[:, 2 * inner_width + 2 * N :]
    raw_mix = jnp.concatenate([values, states], axis=1).astype(jnp.bfloat16)
    tail_rows = from_behind(raw_mix[span_rows - 3 :], "seq", 1)
    extended = jnp.concatenate([tail_rows, raw_mix], axis=0)
    starts = jnp.cumsum(doc_lengths) - doc_lengths
    span_start = seq_index * span_rows
    positions = span_start - 3 + jnp.arange(span_rows + 3, dtype=jnp.int32)
    segment_ext = jnp.sum(starts[None, :] <= positions[:, None], axis=1) - 1
    segment = segment_ext[3:]
    taps = jnp.concatenate(
        [conv_value, lax.dynamic_index_in_dim(conv_state, group_index, 1, keepdims=False)], axis=1
    )
    convolved = jnp.zeros((span_rows, taps.shape[1]), jnp.float32)
    for offset in range(4):
        same_doc = segment_ext[offset : offset + span_rows] == segment
        convolved = (
            convolved
            + jnp.where(
                same_doc[:, None], extended[offset : offset + span_rows].astype(jnp.float32), 0.0
            )
            * taps[offset]
        )
    rounded = lax.optimization_barrier(jax.nn.silu(convolved).astype(jnp.bfloat16))
    activated = rounded.astype(jnp.float32)
    inputs = activated[:, :inner_width].reshape(span_rows, head_count, HEAD_DIM)
    in_map = activated[:, inner_width : inner_width + N]
    out_map = activated[:, inner_width + N :]
    in_half = rounded[:, inner_width : inner_width + N]
    out_half = rounded[:, inner_width + N :]
    step_size = jax.nn.softplus(raw_step + step_bias)
    log_decay = -decay_rate * step_size
    cumulative = jnp.cumsum(log_decay, axis=0)
    order = jnp.arange(span_rows)
    causal = (segment[:, None] == segment[None, :]) & (order[:, None] >= order[None, :])
    gaps = cumulative.T[:, :, None] - cumulative.T[:, None, :]
    decay = jnp.exp(jnp.where(causal[None], gaps, -jnp.inf))
    scores = jnp.dot(out_half, in_half.T, preferred_element_type=jnp.float32)
    mixing = decay * scores[None] * step_size.T[:, None, :]
    intra = jnp.einsum("hts,shp->thp", mixing, inputs, precision=PRECISE)
    last_segment = segment[span_rows - 1]
    prior_segment = segment_ext[2]
    in_last = segment == last_segment
    to_end = (
        jnp.where(in_last[:, None], jnp.exp(cumulative[span_rows - 1][None, :] - cumulative), 0.0)
        * step_size
    )
    local_state = jnp.einsum("sh,shp,sn->hpn", to_end, inputs, in_map, precision=PRECISE)
    passing = jnp.where(last_segment == prior_segment, jnp.exp(cumulative[span_rows - 1]), 0.0)
    empty = jnp.zeros_like(local_state)

    def relay(turn, incoming):
        return from_behind(
            (passing[:, None, None] * incoming + local_state).astype(jnp.bfloat16), "seq", 1
        ).astype(jnp.float32)

    incoming = lax.fori_loop(0, lax.axis_size("seq") - 1, relay, empty)
    carried = jnp.where((segment == prior_segment)[:, None], jnp.exp(cumulative), 0.0)
    from_state = (
        jnp.einsum("tn,hpn->thp", out_map, incoming, precision=PRECISE) * carried[:, :, None]
    )
    outputs = intra + from_state + skip_gain[None, :, None] * inputs
    gated = outputs.reshape(span_rows, inner_width) * jax.nn.silu(gate)
    squares = jnp.sum(gated * gated, axis=1)
    for bit in range(group_devices.bit_length() - 1):
        squares = squares + partner(squares, "fsdp", bit)
    scaled = (
        gated * lax.rsqrt(squares[:, None] / (H * HEAD_DIM // G) + EPSILON) * mix_gain
    ).astype(jnp.bfloat16)
    terms = jnp.dot(
        scaled,
        lax.all_gather(out_proj, "seq", axis=1, tiled=True),
        preferred_element_type=jnp.float32,
    )
    mixed = lax.psum_scatter(
        terms.astype(jnp.bfloat16), "fsdp", scatter_dimension=1, tiled=True
    ).astype(jnp.float32)
    return (tokens.astype(jnp.float32) + mixed).astype(jnp.bfloat16)


VMEM_BYTES = 56 << 20


def swap_cores(value):
    count = lax.axis_size("seq")
    return lax.ppermute(value, "seq", [(place, place ^ 1) for place in range(count)])


def next_chip(value):
    count = lax.axis_size("seq")
    return lax.ppermute(value, "seq", [(place, (place + 2) % count) for place in range(count)])


def flip_fsdp(value, bits):
    count = lax.axis_size("fsdp")
    return lax.ppermute(value, "fsdp", [(place, place ^ bits) for place in range(count)])


def share_of(step, where):
    chips = where[2]
    return 2 * lax.rem(where[0] + chips - step, chips) + where[1]


def value_partials(rows, weights, small, where, chips, width):
    depth = rows.shape[1]
    count, per_share = rows.shape[0], rows.shape[0] // (2 * chips)
    small_width = small.shape[1]
    maps_width = small_width - 128
    assert maps_width == width
    extra = per_share + per_share // 2

    def body(where, rows_ref, weights_ref, small_ref, out_ref):
        share = share_of(pl.program_id(0), where)
        out_ref[0, :count] = jnp.dot(
            rows_ref[...], weights_ref[...], preferred_element_type=jnp.float32
        ).astype(jnp.bfloat16)
        some = rows_ref[pl.ds(pl.multiple_of(share * per_share, per_share), per_share), :]
        thin = jnp.dot(some, small_ref[...], preferred_element_type=jnp.float32).astype(
            jnp.bfloat16
        )
        out_ref[0, count : count + per_share] = thin[:, :maps_width]
        half = per_share // 2
        out_ref[0, count + per_share :] = jnp.concatenate(
            [thin[:half, maps_width:], thin[half:, maps_width:]], axis=1
        )

    return pl.pallas_call(
        body,
        out_shape=jax.ShapeDtypeStruct((chips, count + extra, width), jnp.bfloat16),
        grid_spec=pltpu.PrefetchScalarGridSpec(
            num_scalar_prefetch=1,
            grid=(chips,),
            in_specs=[
                pl.BlockSpec((count, depth), lambda i, where: (0, 0)),
                pl.BlockSpec((depth, width), lambda i, where: (0, share_of(i, where))),
                pl.BlockSpec((depth, small_width), lambda i, where: (0, 0)),
            ],
            out_specs=pl.BlockSpec((1, count + extra, width), lambda i, where: (i, 0, 0)),
        ),
        compiler_params=pltpu.CompilerParams(vmem_limit_bytes=VMEM_BYTES),
        name="value_partials",
    )(where, rows, weights, small)


def gate_partials(pieces, weights, where, chips, width):
    depth = pieces[0].shape[1]
    count = pieces[0].shape[0]

    def body(where, *refs):
        weights_ref, out_ref = refs[-2], refs[-1]
        for place, rows_ref in enumerate(refs[:-2]):
            out_ref[0, place * count : (place + 1) * count] = jnp.dot(
                rows_ref[...], weights_ref[...], preferred_element_type=jnp.float32
            ).astype(jnp.bfloat16)

    return pl.pallas_call(
        body,
        out_shape=jax.ShapeDtypeStruct((chips, len(pieces) * count, width), jnp.bfloat16),
        grid_spec=pltpu.PrefetchScalarGridSpec(
            num_scalar_prefetch=1,
            grid=(chips,),
            in_specs=[pl.BlockSpec((count, depth), lambda i, where: (0, 0)) for _ in pieces]
            + [pl.BlockSpec((depth, width), lambda i, where: (0, share_of(i, where)))],
            out_specs=pl.BlockSpec(
                (1, len(pieces) * count, width), lambda i, where: (i, 0, 0)
            ),
        ),
        compiler_params=pltpu.CompilerParams(vmem_limit_bytes=VMEM_BYTES),
        name="gate_partials",
    )(where, *pieces, weights)


def add_up(*terms):
    total = terms[0].astype(jnp.float32)
    for term in terms[1:]:
        total = total + term.astype(jnp.float32)
    return total


def ring_reduce(kept, lent):
    got = swap_cores(lent)
    chips = kept.shape[0]
    passed = []
    for step in range(1, chips):
        passed = [next_chip(add_up(kept[step], got[step], *passed).astype(jnp.bfloat16))]
    return kept, got, passed[0]


def scan_heads(order, first, second, small, ages, taps, state_taps, bias, rate, skip, sizes):
    stretches, rows, quarters, width = sizes
    span = rows * quarters
    tokens = stretches * span
    count = quarters // 2 * stretches * rows
    per_share = count // stretches
    half = per_share // 2
    heads = width // HEAD_DIM

    def body(order, *refs):
        (k1, g1, r1, k2, g2, r2, small_ref, ages_ref, taps_ref, state_taps_ref, bias_ref) = refs[:11]
        rate_ref, skip_ref, out_ref, values, maps, steps, state = refs[11:]
        first_head = order[quarters]
        values[:8] = jnp.zeros((8, width), jnp.float32)
        maps[:8] = jnp.zeros((8, 2 * N), jnp.float32)

        def place_rows(stretch, carry):
            for k in range(quarters):
                trio = ((k1, g1, r1), (k2, g2, r2))[k // 2]
                at = pl.multiple_of((k % 2) * stretches * rows + stretch * rows, rows)
                to = pl.multiple_of(stretch * span + order[k] * rows, rows)
                total = (
                    trio[0][0, pl.ds(at, rows), :].astype(jnp.float32)
                    + trio[1][0, pl.ds(at, rows), :].astype(jnp.float32)
                    + trio[2][pl.ds(at, rows), :].astype(jnp.float32)
                )
                values[pl.ds(to + 8, rows), :] = total.astype(jnp.bfloat16).astype(jnp.float32)
            return carry

        lax.fori_loop(0, stretches, place_rows, 0)
        for share in range(stretches):
            for group in range(2):
                k = 2 * group + (2 * share) // stretches
                for part in range(2):
                    stretch = (2 * share) % stretches + part
                    to = pl.multiple_of(stretch * span + order[k] * rows, rows)
                    maps[pl.ds(to + 8, rows), :] = small_ref[
                        share, group, part * half : (part + 1) * half
                    ].astype(jnp.float32)
                    steps[pl.ds(to, rows), :] = small_ref[
                        share, group, per_share:, part * 128 : (part + 1) * 128
                    ].astype(jnp.float32)
        state[...] = jnp.zeros_like(state)
        row = lax.broadcasted_iota(jnp.int32, (span, span), 0)
        gap = row - lax.broadcasted_iota(jnp.int32, (span, span), 1)
        lower = jnp.where(gap >= 0, 1.0, 0.0)
        here = lax.broadcasted_iota(jnp.int32, (span, 1), 0)
        head_of = lax.broadcasted_iota(jnp.int32, (1, width), 1) // HEAD_DIM

        def by_head(columns):
            wide = jnp.broadcast_to(columns[:, 0:1], (columns.shape[0], width))
            for head in range(1, heads):
                wide = jnp.where(head_of == head, columns[:, head : head + 1], wide)
            return wide

        def convolve(source, gains, start, age):
            block = source[pl.ds(start, span + 8), :]
            total = block[8:] * gains[3:4]
            for lag in range(1, 4):
                total = total + jnp.where(age >= lag, block[8 - lag : 8 - lag + span], 0.0) * gains[
                    3 - lag : 4 - lag
                ]
            return (total * jax.nn.sigmoid(total)).astype(jnp.bfloat16)

        def chunk(index, carry):
            start = pl.multiple_of(index * span, span)
            age = ages_ref[pl.ds(start, span), :]
            last_age = age[span - 1 :]
            inputs = convolve(values, taps_ref[...], start, age)
            both = convolve(maps, state_taps_ref[...], start, age)
            in_map, out_map = both[:, :N], both[:, N:]
            raw = pltpu.roll(steps[pl.ds(start, span), :], lax.rem(128 - first_head, 128), 1)
            raw = raw + bias_ref[...]
            size = jnp.maximum(raw, 0.0) + jnp.log1p(jnp.exp(-jnp.abs(raw)))
            total = jnp.dot(
                lower,
                -rate_ref[...] * size,
                precision=PRECISE,
                preferred_element_type=jnp.float32,
            )
            total_rows, size_rows = total.T, size.T
            scores = lax.dot_general(
                out_map, in_map, (((1,), (1,)), ((), ())), preferred_element_type=jnp.float32
            )
            near = (gap >= 0) & (gap <= age)
            history = jnp.zeros((span, width), jnp.float32)
            for head in range(heads):
                decay = jnp.exp(
                    jnp.where(
                        near, total[:, head : head + 1] - total_rows[head : head + 1], -jnp.inf
                    )
                )
                mixing = (decay * scores * size_rows[head : head + 1]).astype(jnp.bfloat16)
                part = jnp.dot(mixing, inputs, preferred_element_type=jnp.float32)
                history = jnp.where(head_of == head, part, history)
            old = state[...]
            carried = by_head(jnp.where(age > here, jnp.exp(total), 0.0))
            history = history + carried * jnp.dot(
                out_map, old.astype(jnp.bfloat16), preferred_element_type=jnp.float32
            )
            wide = inputs.astype(jnp.float32)
            out_ref[pl.ds(start, span), :] = history + skip_ref[...] * wide
            end = total[span - 1 :]
            to_end = by_head(
                jnp.where(span - 1 - here <= last_age, jnp.exp(end - total), 0.0) * size
            )
            keep = by_head(jnp.where(last_age >= span, jnp.exp(end), 0.0))
            state[...] = keep * old + lax.dot_general(
                in_map,
                (wide * to_end).astype(jnp.bfloat16),
                (((0,), (0,)), ((), ())),
                preferred_element_type=jnp.float32,
            )
            return carry

        lax.fori_loop(0, stretches, chunk, 0)

    whole = lambda shape: pl.BlockSpec(shape, lambda i, order: (0,) * len(shape))
    trio_specs = [
        whole((1,) + first[0].shape[1:]),
        whole((1,) + first[0].shape[1:]),
        whole(first[2].shape),
    ]
    rest = (small, ages, taps, state_taps, bias, rate, skip)
    return pl.pallas_call(
        body,
        out_shape=jax.ShapeDtypeStruct((tokens, width), jnp.float32),
        grid_spec=pltpu.PrefetchScalarGridSpec(
            num_scalar_prefetch=1,
            grid=(1,),
            in_specs=trio_specs + trio_specs + [whole(value.shape) for value in rest],
            out_specs=whole((tokens, width)),
            scratch_shapes=[
                pltpu.VMEM((tokens + 8, width), jnp.float32),
                pltpu.VMEM((tokens + 8, 2 * N), jnp.float32),
                pltpu.VMEM((tokens, 128), jnp.float32),
                pltpu.VMEM((N, width), jnp.float32),
            ],
        ),
        compiler_params=pltpu.CompilerParams(vmem_limit_bytes=VMEM_BYTES),
        name="scan_heads",
    )(order, *first, *second, *rest)


def gate_outputs(order, outputs, trio, sizes):
    stretches, rows, quarters, width = sizes
    chips = trio[0].shape[0]
    kept, got = (value.reshape(chips, quarters, stretches, rows, width) for value in trio[:2])
    last = trio[2].reshape(quarters, stretches, rows, width)

    def body(order, outputs_ref, kept_ref, got_ref, last_ref, out_ref):
        gate = (
            kept_ref[0, 0].astype(jnp.float32)
            + got_ref[0, 0].astype(jnp.float32)
            + last_ref[0].astype(jnp.float32)
        )
        out_ref[:, 0] = (outputs_ref[:, 0] * gate * jax.nn.sigmoid(gate)).astype(jnp.bfloat16)

    part = pl.BlockSpec(
        (1, 1, stretches, rows, width), lambda q, order: (0, order[q], 0, 0, 0)
    )
    natural = pl.BlockSpec((stretches, 1, rows, width), lambda q, order: (0, q, 0, 0))
    return pl.pallas_call(
        body,
        out_shape=jax.ShapeDtypeStruct((stretches, quarters, rows, width), jnp.bfloat16),
        grid_spec=pltpu.PrefetchScalarGridSpec(
            num_scalar_prefetch=1,
            grid=(quarters,),
            in_specs=[
                natural,
                part,
                part,
                pl.BlockSpec(
                    (1, stretches, rows, width), lambda q, order: (order[q], 0, 0, 0)
                ),
            ],
            out_specs=natural,
        ),
        compiler_params=pltpu.CompilerParams(vmem_limit_bytes=VMEM_BYTES),
        name="gate_outputs",
    )(order, outputs.reshape(stretches, quarters, rows, width), kept, got, last)


def mix_channels(where, blocks, gains, weights, sizes):
    stretches, rows, quarters, width = sizes
    span = rows * quarters
    columns = weights.shape[1]
    channels = weights.shape[0]

    def body(where, *refs):
        block_refs, (gains_ref, weights_ref, out_ref) = refs[:-3], refs[-3:]
        squares = jnp.zeros((span, 1), jnp.float32)
        for block_ref in block_refs:
            block = block_ref[...].astype(jnp.float32)
            squares = squares + jnp.sum(block * block, axis=1, keepdims=True)
        factor = lax.rsqrt(squares / channels + EPSILON)
        total = jnp.zeros((span, columns), jnp.float32)
        for place, block_ref in enumerate(block_refs):
            owner = share_of(place // 2, where)
            owner = owner if place % 2 == 0 else owner + 1 - 2 * where[1]
            at = pl.multiple_of(owner * width, width)
            scaled = (
                block_ref[...].astype(jnp.float32) * factor * gains_ref[pl.ds(owner, 1), :]
            ).astype(jnp.bfloat16)
            total = total + jnp.dot(
                scaled, weights_ref[pl.ds(at, width), :], preferred_element_type=jnp.float32
            )
        total = total.astype(jnp.bfloat16)
        for quarter in range(quarters):
            out_ref[quarter, 0] = total[quarter * rows : (quarter + 1) * rows]

    return pl.pallas_call(
        body,
        out_shape=jax.ShapeDtypeStruct((quarters, stretches, rows, columns), jnp.bfloat16),
        grid_spec=pltpu.PrefetchScalarGridSpec(
            num_scalar_prefetch=1,
            grid=(stretches,),
            in_specs=[pl.BlockSpec((span, width), lambda t, where: (t, 0)) for _ in blocks]
            + [
                pl.BlockSpec(gains.shape, lambda t, where: (0, 0)),
                pl.BlockSpec(weights.shape, lambda t, where: (0, 0)),
            ],
            out_specs=pl.BlockSpec(
                (quarters, 1, rows, columns), lambda t, where: (0, t, 0, 0)
            ),
        ),
        compiler_params=pltpu.CompilerParams(vmem_limit_bytes=VMEM_BYTES),
        name="mix_channels",
    )(where, *blocks, gains, weights)


def by_channel(
    tokens,
    norm_gain,
    gate_proj,
    value_proj,
    step_proj,
    state_proj,
    conv_value,
    conv_state,
    step_bias,
    decay_rate,
    skip_gain,
    mix_gain,
    out_proj,
    doc_lengths,
):
    stretches = lax.axis_size("seq")
    quarters = lax.axis_size("fsdp")
    chips = stretches // 2
    span, features = tokens.shape
    rows = span // quarters
    depth, inner_width = gate_proj.shape
    width = inner_width // stretches
    head_count = step_bias.shape[0]
    heads = head_count // stretches
    total_tokens = stretches * span
    sizes = (stretches, rows, quarters, width)
    seq_index = lax.axis_index("seq")
    fsdp_index = lax.axis_index("fsdp")
    chip, core = seq_index // 2, seq_index % 2
    place = lambda core_index: jnp.stack([chip, core_index, jnp.full_like(chip, chips)])
    mine, other = place(core), place(1 - core)
    order = jnp.stack(
        [fsdp_index ^ k for k in range(quarters)] + [(seq_index * heads).astype(jnp.int32)]
    )

    state_cols = lax.dynamic_index_in_dim(state_proj, fsdp_index, 1, keepdims=False)
    small = jnp.concatenate(
        [state_cols, step_proj, jnp.zeros((depth, 128 - head_count), jnp.bfloat16)], axis=1
    )
    starts = jnp.cumsum(doc_lengths) - doc_lengths
    index = jnp.arange(total_tokens, dtype=jnp.int32)[:, None]
    ages = jnp.min(
        jnp.where(starts[None, :] <= index, index - starts[None, :], total_tokens),
        axis=1,
        keepdims=True,
    )
    own_part = lambda value: lax.dynamic_slice_in_dim(value, seq_index * heads, heads, 0)
    lanes = lambda value: jnp.pad(own_part(value), (0, 128 - heads))[None, :]
    bias, rate = lanes(step_bias), lanes(decay_rate)
    skip = jnp.repeat(own_part(skip_gain), HEAD_DIM)[None, :]
    taps = lax.dynamic_slice_in_dim(conv_value, seq_index * width, width, 1)
    state_taps = lax.dynamic_index_in_dim(conv_state, fsdp_index, 1, keepdims=False)

    parts = lax.all_to_all(
        tokens.reshape(quarters, rows, features), "fsdp", split_axis=0, concat_axis=0, tiled=True
    )
    as_float = parts.astype(jnp.float32)
    mean_square = jnp.sum(as_float * as_float, axis=(0, 2), keepdims=True) / (
        quarters * features
    )
    normed = (
        as_float * lax.rsqrt(mean_square + EPSILON) * norm_gain.reshape(quarters, 1, features)
    ).astype(jnp.bfloat16)
    slices = (
        normed.reshape(quarters, rows, stretches // quarters, depth)
        .transpose(0, 2, 1, 3)
        .reshape(stretches, rows, depth)
    )
    own = lax.all_to_all(slices, "seq", split_axis=0, concat_axis=0, tiled=True).reshape(
        stretches * rows, depth
    )
    pieces = [own] + [flip_fsdp(own, k) for k in range(1, quarters)]
    pair = lambda a, b: jnp.concatenate([pieces[a], pieces[b]], axis=0)
    early, late = pair(0, 1), pair(2, 3)

    def reduced_values(rows_in):
        lent = value_partials(rows_in, value_proj, small, other, chips, width)
        kept = value_partials(rows_in, value_proj, small, mine, chips, width)
        return ring_reduce(kept, lent)

    first = reduced_values(early)
    second = reduced_values(late)
    gates = ring_reduce(
        gate_partials([early, late], gate_proj, mine, chips, width),
        gate_partials([early, late], gate_proj, other, chips, width),
    )
    count = early.shape[0]
    thin = jnp.stack(
        [
            add_up(trio[0][0, count:], trio[1][0, count:], trio[2][count:]).astype(jnp.bfloat16)
            for trio in (first, second)
        ]
    )
    thin = lax.all_gather(thin, "seq", axis=0)
    outputs = scan_heads(
        order, first, second, thin, ages, taps, state_taps, bias, rate, skip, sizes
    )
    gated = gate_outputs(order, outputs, gates, sizes).reshape(total_tokens, width)
    blocks = []
    for step in range(chips):
        blocks += [gated, swap_cores(gated)]
        if step + 1 < chips:
            gated = next_chip(gated)
    terms = mix_channels(
        mine, blocks, mix_gain.reshape(stretches, width), out_proj, sizes
    )
    split = terms.shape[3] // 2
    near = [lax.dynamic_index_in_dim(terms, fsdp_index ^ k, 0, keepdims=False) for k in range(4)]
    left = [value[..., :split] for value in near]
    right = [value[..., split:] for value in near]
    left_got = flip_fsdp(jnp.stack([left[1], left[3]]), 1)
    right_got = flip_fsdp(jnp.stack([right[2], right[3]]), 2)
    left_more = flip_fsdp(add_up(left[2], left_got[1]).astype(jnp.bfloat16), 2)
    right_more = flip_fsdp(add_up(right[1], right_got[1]).astype(jnp.bfloat16), 1)
    summed = jnp.concatenate(
        [
            add_up(left[0], left_got[0], left_more).astype(jnp.bfloat16),
            add_up(right[0], right_got[0], right_more).astype(jnp.bfloat16),
        ],
        axis=2,
    )
    moved = lax.all_to_all(summed, "seq", split_axis=0, concat_axis=0, tiled=True)
    moved = lax.all_to_all(moved, "fsdp", split_axis=0, concat_axis=0, tiled=True)
    mixed = (
        moved.reshape(quarters, stretches // quarters, rows, depth)
        .transpose(0, 2, 1, 3)
        .reshape(span, features)
    )
    return (tokens.astype(jnp.float32) + mixed.astype(jnp.float32)).astype(jnp.bfloat16)


def layer(*arguments):
    stretches, quarters = lax.axis_size("seq"), lax.axis_size("fsdp")
    span, inner_width = arguments[0].shape[0], arguments[2].shape[1]
    heads = arguments[8].shape[0]
    width = inner_width // stretches
    aligned = (
        quarters == G
        and quarters == 4
        and stretches % (2 * quarters) == 0
        and width == 2 * N
        and width % HEAD_DIM == 0
        and heads <= 128
        and span % (16 * quarters) == 0
        and span % 128 == 0
    )
    return (by_channel if aligned else by_stretch)(*arguments)


def solution(mesh):
    return jax.shard_map(
        layer,
        mesh=mesh,
        in_specs=(
            P("seq", "fsdp"),
            P(),
            P("seq", "fsdp"),
            P("seq", "fsdp"),
            P("seq", "fsdp"),
            P("seq", None, None),
            P(None, "fsdp"),
            P(),
            P("fsdp"),
            P("fsdp"),
            P("fsdp"),
            P("fsdp"),
            P("fsdp", "seq"),
            P(),
        ),
        out_specs=P("seq", "fsdp"),
        check_vma=False,
    )
```

```python
import jax
import jax.numpy as jnp
from jax import lax
from jax.experimental import pallas as pl
from jax.experimental.pallas import tpu as pltpu
from jax.sharding import PartitionSpec as P

H = 128
HEAD_DIM = 64
N = 128
G = 4


EPSILON = 1e-05
PRECISE = lax.Precision.HIGHEST


def from_behind(value, axis, steps):
    count = lax.axis_size(axis)
    leading, last = (max(0, -steps), min(count, count - steps))
    return lax.ppermute(value, axis, [(source, source + steps) for source in range(leading, last)])


def partner(block, axis, distance):
    count = lax.axis_size(axis)
    route = []
    for low in range(count):
        high = low | 1 << distance
        if high != low and high < count:
            route += [(low, high), (high, low)]
    return lax.ppermute(block, axis, route)


def by_stretch(
    tokens,
    norm_gain,
    gate_proj,
    value_proj,
    step_proj,
    state_proj,
    conv_value,
    conv_state,
    step_bias,
    decay_rate,
    skip_gain,
    mix_gain,
    out_proj,
    doc_lengths,
):
    span_rows = tokens.shape[0]
    seq_index = lax.axis_index("seq")
    fsdp_index = lax.axis_index("fsdp")
    head_count = step_bias.shape[0]
    inner_width = gate_proj.shape[1]
    group_devices = lax.axis_size("fsdp") // G
    group_index = fsdp_index // group_devices
    gathered = lax.all_gather(tokens, "fsdp", axis=1, tiled=True)
    as_float = gathered.astype(jnp.float32)
    normed = (
        as_float
        * lax.rsqrt(jnp.mean(as_float * as_float, axis=1, keepdims=True) + EPSILON)
        * norm_gain
    ).astype(jnp.bfloat16)
    state_cols = lax.dynamic_index_in_dim(state_proj, group_index, 1, keepdims=False)
    stacked = jnp.concatenate([gate_proj, value_proj, state_cols, step_proj], axis=1)
    spread = lax.all_to_all(normed, "seq", split_axis=1, concat_axis=0, tiled=True)
    summed = lax.psum_scatter(
        jnp.dot(spread, stacked, preferred_element_type=jnp.float32),
        "seq",
        scatter_dimension=0,
        tiled=True,
    )
    gate = summed[:, :inner_width]
    values = summed[:, inner_width : 2 * inner_width]
    states = summed[:, 2 * inner_width : 2 * inner_width + 2 * N]
    raw_step = summed[:, 2 * inner_width + 2 * N :]
    raw_mix = jnp.concatenate([values, states], axis=1).astype(jnp.bfloat16)
    tail_rows = from_behind(raw_mix[span_rows - 3 :], "seq", 1)
    extended = jnp.concatenate([tail_rows, raw_mix], axis=0)
    starts = jnp.cumsum(doc_lengths) - doc_lengths
    span_start = seq_index * span_rows
    positions = span_start - 3 + jnp.arange(span_rows + 3, dtype=jnp.int32)
    segment_ext = jnp.sum(starts[None, :] <= positions[:, None], axis=1) - 1
    segment = segment_ext[3:]
    taps = jnp.concatenate(
        [conv_value, lax.dynamic_index_in_dim(conv_state, group_index, 1, keepdims=False)], axis=1
    )
    convolved = jnp.zeros((span_rows, taps.shape[1]), jnp.float32)
    for offset in range(4):
        same_doc = segment_ext[offset : offset + span_rows] == segment
        convolved = (
            convolved
            + jnp.where(
                same_doc[:, None], extended[offset : offset + span_rows].astype(jnp.float32), 0.0
            )
            * taps[offset]
        )
    rounded = lax.optimization_barrier(jax.nn.silu(convolved).astype(jnp.bfloat16))
    activated = rounded.astype(jnp.float32)
    inputs = activated[:, :inner_width].reshape(span_rows, head_count, HEAD_DIM)
    in_map = activated[:, inner_width : inner_width + N]
    out_map = activated[:, inner_width + N :]
    in_half = rounded[:, inner_width : inner_width + N]
    out_half = rounded[:, inner_width + N :]
    step_size = jax.nn.softplus(raw_step + step_bias)
    log_decay = -decay_rate * step_size
    cumulative = jnp.cumsum(log_decay, axis=0)
    order = jnp.arange(span_rows)
    causal = (segment[:, None] == segment[None, :]) & (order[:, None] >= order[None, :])
    gaps = cumulative.T[:, :, None] - cumulative.T[:, None, :]
    decay = jnp.exp(jnp.where(causal[None], gaps, -jnp.inf))
    scores = jnp.dot(out_half, in_half.T, preferred_element_type=jnp.float32)
    mixing = decay * scores[None] * step_size.T[:, None, :]
    intra = jnp.einsum("hts,shp->thp", mixing, inputs, precision=PRECISE)
    last_segment = segment[span_rows - 1]
    prior_segment = segment_ext[2]
    in_last = segment == last_segment
    to_end = (
        jnp.where(in_last[:, None], jnp.exp(cumulative[span_rows - 1][None, :] - cumulative), 0.0)
        * step_size
    )
    local_state = jnp.einsum("sh,shp,sn->hpn", to_end, inputs, in_map, precision=PRECISE)
    passing = jnp.where(last_segment == prior_segment, jnp.exp(cumulative[span_rows - 1]), 0.0)
    empty = jnp.zeros_like(local_state)

    def relay(turn, incoming):
        return from_behind(
            (passing[:, None, None] * incoming + local_state).astype(jnp.bfloat16), "seq", 1
        ).astype(jnp.float32)

    incoming = lax.fori_loop(0, lax.axis_size("seq") - 1, relay, empty)
    carried = jnp.where((segment == prior_segment)[:, None], jnp.exp(cumulative), 0.0)
    from_state = (
        jnp.einsum("tn,hpn->thp", out_map, incoming, precision=PRECISE) * carried[:, :, None]
    )
    outputs = intra + from_state + skip_gain[None, :, None] * inputs
    gated = outputs.reshape(span_rows, inner_width) * jax.nn.silu(gate)
    squares = jnp.sum(gated * gated, axis=1)
    for bit in range(group_devices.bit_length() - 1):
        squares = squares + partner(squares, "fsdp", bit)
    scaled = (
        gated * lax.rsqrt(squares[:, None] / (H * HEAD_DIM // G) + EPSILON) * mix_gain
    ).astype(jnp.bfloat16)
    terms = jnp.dot(
        scaled,
        lax.all_gather(out_proj, "seq", axis=1, tiled=True),
        preferred_element_type=jnp.float32,
    )
    mixed = lax.psum_scatter(
        terms.astype(jnp.bfloat16), "fsdp", scatter_dimension=1, tiled=True
    ).astype(jnp.float32)
    return (tokens.astype(jnp.float32) + mixed).astype(jnp.bfloat16)


VMEM_BYTES = 56 << 20


def swap_cores(value):
    count = lax.axis_size("seq")
    return lax.ppermute(value, "seq", [(place, place ^ 1) for place in range(count)])


def next_chip(value, away=1):
    count = lax.axis_size("seq")
    route = [(place, (place + 2 * away) % count) for place in range(count)]
    return lax.ppermute(value, "seq", route)


def flip_fsdp(value, bits):
    count = lax.axis_size("fsdp")
    return lax.ppermute(value, "fsdp", [(place, place ^ bits) for place in range(count)])


def share_partials(pieces, value_proj, gate_proj, small, where, chips, width):
    depth, count = pieces[0].shape[1], pieces[0].shape[0]
    rows = count // (2 * chips)
    number = len(pieces)
    tall = number * count
    projections = [value for value in (value_proj, gate_proj) if value is not None]
    thin_inputs = [] if small is None else [small]
    thin_rows = 0 if small is None else number * (rows + rows // 2)
    thin_width = 128 if small is None else small.shape[1]
    total_rows = len(projections) * tall + thin_rows

    def body(where, *refs):
        row_refs, refs = refs[:number], refs[number:]
        weight_refs, refs = refs[: len(projections)], refs[len(projections) :]
        lent_ref, kept_ref, thin = refs[-3:]
        index, core = pl.program_id(0), where[1]
        chip = lax.rem(where[0] + chips - index, chips)
        first = core == 0

        if small is not None:

            @pl.when(index == 0)
            def _():
                for place in range(number):
                    thin[place * count : (place + 1) * count] = jnp.dot(
                        row_refs[place][...], refs[0][...], preferred_element_type=jnp.float32
                    ).astype(jnp.bfloat16)

            for out_ref, own in ((lent_ref, 1 - core), (kept_ref, core)):
                for place in range(number):
                    at = place * count + (own * chips + chip) * rows
                    to = tall + place * rows
                    out_ref[0, to : to + rows] = thin[
                        pl.ds(pl.multiple_of(at, rows), rows), : thin_width - 128
                    ]
                    to = tall + number * rows + place * rows // 2
                    halves = [
                        thin[
                            pl.ds(pl.multiple_of(at + part * rows // 2, rows // 2), rows // 2),
                            thin_width - 128 :,
                        ]
                        for part in range(2)
                    ]
                    out_ref[0, to : to + rows // 2] = jnp.concatenate(halves, axis=1)

        for which, weight_ref in enumerate(weight_refs):
            base = which * (tall + thin_rows)
            for place in range(number):
                both = jnp.dot(
                    row_refs[place][...], weight_ref[...], preferred_element_type=jnp.float32
                ).astype(jnp.bfloat16)
                at = slice(base + place * count, base + (place + 1) * count)
                kept_ref[0, at] = jnp.where(first, both[:, :width], both[:, width:])
                lent_ref[0, at] = jnp.where(first, both[:, width:], both[:, :width])

    out = jax.ShapeDtypeStruct((chips, total_rows, width), jnp.bfloat16)
    return pl.pallas_call(
        body,
        out_shape=[out, out],
        grid_spec=pltpu.PrefetchScalarGridSpec(
            num_scalar_prefetch=1,
            grid=(chips,),
            in_specs=[pl.BlockSpec((count, depth), lambda i, where: (0, 0)) for _ in pieces]
            + [
                pl.BlockSpec(
                    (depth, 2 * width), lambda i, where: (0, lax.rem(where[0] + chips - i, chips))
                )
                for _ in projections
            ]
            + [pl.BlockSpec(value.shape, lambda i, where: (0, 0)) for value in thin_inputs],
            out_specs=[pl.BlockSpec((1, total_rows, width), lambda i, where: (i, 0, 0))] * 2,
            scratch_shapes=[
                pltpu.VMEM((16 if small is None else tall, thin_width), jnp.bfloat16)
            ],
        ),
        compiler_params=pltpu.CompilerParams(vmem_limit_bytes=VMEM_BYTES),
        name="share_partials",
    )(where, *pieces, *projections, *thin_inputs)


def add_up(*terms):
    total = terms[0].astype(jnp.float32)
    for term in terms[1:]:
        total = total + term.astype(jnp.float32)
    return total


def ring_reduce(kept, lent):
    got = swap_cores(lent)
    chips = kept.shape[0]
    passed = []
    for step in range(1, chips):
        sent = add_up(kept[step], got[step], *passed).astype(jnp.bfloat16)
        passed = [next_chip(sent)]
    return kept, got, passed[0]


def scan_heads(order, trios, groups, thin, thin_swapped, ages, taps, state_taps, bias, rate, skip, sizes):
    stretches, rows, quarters, width = sizes
    span = rows * quarters
    tokens = stretches * span
    count = stretches * rows
    half = rows // 2
    chips = stretches // 2
    heads = width // HEAD_DIM
    flat = [value for trio in trios for value in trio]
    number = len(flat)

    def body(order, *refs):
        trio_refs, refs = refs[:number], refs[number:]
        thin_ref, swapped_ref, ages_ref, taps_ref, state_taps_ref, bias_ref = refs[:6]
        rate_ref, skip_ref, out_ref, values, maps, steps, state = refs[6:]
        first_head, chip, core = (order[quarters + place] for place in range(3))
        values[:8] = jnp.zeros((8, width), jnp.float32)
        maps[:8] = jnp.zeros((8, 2 * N), jnp.float32)

        def place_rows(stretch, carry):
            for group, members in enumerate(groups):
                kept, got, last = trio_refs[3 * group : 3 * group + 3]
                for place, k in enumerate(members):
                    at = pl.multiple_of(place * count + stretch * rows, rows)
                    to = pl.multiple_of(stretch * span + order[k] * rows, rows)
                    total = (
                        kept[0, pl.ds(at, rows), :].astype(jnp.float32)
                        + got[0, pl.ds(at, rows), :].astype(jnp.float32)
                        + last[pl.ds(at, rows), :].astype(jnp.float32)
                    )
                    values[pl.ds(to + 8, rows), :] = total.astype(jnp.bfloat16).astype(
                        jnp.float32
                    )
            return carry

        lax.fori_loop(0, stretches, place_rows, 0)
        for source, own_core in ((thin_ref, core), (swapped_ref, 1 - core)):
            for away in range(chips):
                stretch = own_core * chips + lax.rem(chip + chips - away, chips)
                base = 0
                for members in groups:
                    for place, k in enumerate(members):
                        to = pl.multiple_of(stretch * span + order[k] * rows, rows)
                        at = base + place * rows
                        maps[pl.ds(to + 8, rows), :] = source[away, at : at + rows].astype(
                            jnp.float32
                        )
                        at = base + len(members) * rows + place * half
                        for part in range(2):
                            steps[pl.ds(pl.multiple_of(to + part * half, half), half), :] = source[
                                away, at : at + half, part * 128 : (part + 1) * 128
                            ].astype(jnp.float32)
                    base += len(members) * (rows + half)
        state[...] = jnp.zeros_like(state)
        row = lax.broadcasted_iota(jnp.int32, (span, span), 0)
        gap = row - lax.broadcasted_iota(jnp.int32, (span, span), 1)
        lower = jnp.where(gap >= 0, 1.0, 0.0)
        here = lax.broadcasted_iota(jnp.int32, (span, 1), 0)
        head_of = lax.broadcasted_iota(jnp.int32, (1, width), 1) // HEAD_DIM

        def by_head(columns):
            wide = jnp.broadcast_to(columns[:, 0:1], (columns.shape[0], width))
            for head in range(1, heads):
                wide = jnp.where(head_of == head, columns[:, head : head + 1], wide)
            return wide

        def convolve(source, gains, start, age):
            block = source[pl.ds(start, span + 8), :]
            total = block[8:] * gains[3:4]
            for lag in range(1, 4):
                total = total + jnp.where(age >= lag, block[8 - lag : 8 - lag + span], 0.0) * gains[
                    3 - lag : 4 - lag
                ]
            return (total * jax.nn.sigmoid(total)).astype(jnp.bfloat16)

        def chunk(index, carry):
            start = pl.multiple_of(index * span, span)
            age = ages_ref[pl.ds(start, span), :]
            last_age = age[span - 1 :]
            inputs = convolve(values, taps_ref[...], start, age)
            both = convolve(maps, state_taps_ref[...], start, age)
            in_map, out_map = both[:, :N], both[:, N:]
            raw = pltpu.roll(steps[pl.ds(start, span), :], lax.rem(128 - first_head, 128), 1)
            raw = raw + bias_ref[...]
            size = jnp.maximum(raw, 0.0) + jnp.log1p(jnp.exp(-jnp.abs(raw)))
            total = jnp.dot(
                lower,
                -rate_ref[...] * size,
                precision=PRECISE,
                preferred_element_type=jnp.float32,
            )
            total_rows, size_rows = total.T, size.T
            scores = lax.dot_general(
                out_map, in_map, (((1,), (1,)), ((), ())), preferred_element_type=jnp.float32
            )
            near = (gap >= 0) & (gap <= age)
            history = jnp.zeros((span, width), jnp.float32)
            for head in range(heads):
                decay = jnp.exp(
                    jnp.where(
                        near, total[:, head : head + 1] - total_rows[head : head + 1], -jnp.inf
                    )
                )
                mixing = (decay * scores * size_rows[head : head + 1]).astype(jnp.bfloat16)
                part = jnp.dot(mixing, inputs, preferred_element_type=jnp.float32)
                history = jnp.where(head_of == head, part, history)
            old = state[...]
            carried = by_head(jnp.where(age > here, jnp.exp(total), 0.0))
            history = history + carried * jnp.dot(
                out_map, old.astype(jnp.bfloat16), preferred_element_type=jnp.float32
            )
            wide = inputs.astype(jnp.float32)
            out_ref[pl.ds(start, span), :] = history + skip_ref[...] * wide
            end = total[span - 1 :]
            to_end = by_head(
                jnp.where(span - 1 - here <= last_age, jnp.exp(end - total), 0.0) * size
            )
            keep = by_head(jnp.where(last_age >= span, jnp.exp(end), 0.0))
            state[...] = keep * old + lax.dot_general(
                in_map,
                (wide * to_end).astype(jnp.bfloat16),
                (((0,), (0,)), ((), ())),
                preferred_element_type=jnp.float32,
            )
            return carry

        lax.fori_loop(0, stretches, chunk, 0)

    whole = lambda value: pl.BlockSpec(value.shape, lambda i, order: (0,) * value.ndim)
    trio_specs = [
        pl.BlockSpec((1,) + value.shape[1:], lambda i, order: (0, 0, 0))
        if value.ndim == 3
        else whole(value)
        for value in flat
    ]
    rest = (thin, thin_swapped, ages, taps, state_taps, bias, rate, skip)
    return pl.pallas_call(
        body,
        out_shape=jax.ShapeDtypeStruct((tokens, width), jnp.float32),
        grid_spec=pltpu.PrefetchScalarGridSpec(
            num_scalar_prefetch=1,
            grid=(1,),
            in_specs=trio_specs + [whole(value) for value in rest],
            out_specs=pl.BlockSpec((tokens, width), lambda i, order: (0, 0)),
            scratch_shapes=[
                pltpu.VMEM((tokens + 8, width), jnp.float32),
                pltpu.VMEM((tokens + 8, 2 * N), jnp.float32),
                pltpu.VMEM((tokens, 128), jnp.float32),
                pltpu.VMEM((N, width), jnp.float32),
            ],
        ),
        compiler_params=pltpu.CompilerParams(vmem_limit_bytes=VMEM_BYTES),
        name="scan_heads",
    )(order, *flat, *rest)


def gate_outputs(order, outputs, trios, groups, offsets, sizes):
    stretches, rows, quarters, width = sizes
    count, half, chips = stretches * rows, rows // 2, stretches // 2
    flat = [value for trio in trios for value in trio]
    number = len(flat)

    def body(order, *refs):
        trio_refs, outputs_ref, parts = refs[:number], refs[number], refs[number + 1 :]
        core = order[quarters + 2]

        def one_chip(chip, carry):
            for role, stretch in enumerate((2 * chip + core, 2 * chip + 1 - core)):
                for group, members in enumerate(groups):
                    kept, got, last = trio_refs[3 * group : 3 * group + 3]
                    for place, k in enumerate(members):
                        at = offsets[group] + place * count + stretch * rows
                        at = pl.ds(pl.multiple_of(at, 16), rows)
                        gate = (
                            kept[0, at, :].astype(jnp.float32)
                            + got[0, at, :].astype(jnp.float32)
                            + last[at, :].astype(jnp.float32)
                        )
                        value = (
                            outputs_ref[stretch, order[k]] * gate * jax.nn.sigmoid(gate)
                        ).astype(jnp.bfloat16)
                        for part in range(2):
                            parts[2 * role + part][chip, order[k]] = value[
                                part * half : (part + 1) * half
                            ]
            return carry

        lax.fori_loop(0, chips, one_chip, 0)

    whole = lambda shape: pl.BlockSpec(shape, lambda i, order: (0,) * len(shape))
    shape = (chips, quarters, half, width)
    return pl.pallas_call(
        body,
        out_shape=[jax.ShapeDtypeStruct(shape, jnp.bfloat16)] * 4,
        grid_spec=pltpu.PrefetchScalarGridSpec(
            num_scalar_prefetch=1,
            grid=(1,),
            in_specs=[
                whole((1,) + value.shape[1:] if value.ndim == 3 else value.shape)
                for value in flat
            ]
            + [whole((stretches, quarters, rows, width))],
            out_specs=[whole(shape)] * 4,
        ),
        compiler_params=pltpu.CompilerParams(vmem_limit_bytes=VMEM_BYTES),
        name="gate_outputs",
    )(order, *flat, outputs.reshape(stretches, quarters, rows, width))


def mix_channels(order, near, far, away, so_far, gains, own_proj, other_proj, sizes):
    stretches, rows, quarters, width = sizes
    half, chips = rows // 2, stretches // 2
    count = near.shape[1]
    channels, columns = own_proj.shape
    last = so_far is not None
    so_far = list(so_far) if last else []

    def owner_of(i, order):
        chip, core = order[quarters + 1], order[quarters + 2]
        return 2 * lax.rem(chip + chips - away - i // 2, chips) + lax.rem(core + i, 2)

    def body(order, near_ref, far_ref, gains_ref, own_ref, other_ref, *refs):
        before, refs = refs[: len(so_far)], refs[len(so_far) :]
        total, squares = refs[-2:] if last else refs
        index = pl.program_id(0)

        @pl.when(index == 0)
        def _():
            total[...] = before[0][...] if last else jnp.zeros_like(total)
            squares[...] = before[1][...] if last else jnp.zeros_like(squares)

        block = jnp.where(index < 2, near_ref[0], far_ref[0]).astype(jnp.float32)
        squares[...] += jnp.broadcast_to(
            jnp.sum(block * block, axis=1, keepdims=True), squares.shape
        )
        gained = (block * gains_ref[pl.ds(owner_of(index, order), 1), :]).astype(jnp.bfloat16)
        for side, weights_ref in enumerate((own_ref, other_ref)):
            total[:, side * columns : (side + 1) * columns] += jnp.dot(
                gained, weights_ref[...], preferred_element_type=jnp.float32
            )
        if last:
            rounded = refs[4]

            @pl.when(index == pl.num_programs(0) - 1)
            def _():
                factor = lax.rsqrt(squares[:, :1] / channels + EPSILON)
                rounded[...] = (total[...] * factor).astype(jnp.bfloat16)
                left_kept, left_sent, right_kept, right_sent = refs[:4]
                for k in range(4):
                    for chip in range(chips):
                        at = pl.multiple_of((chip * quarters + order[k]) * half, half)
                        value = rounded[pl.ds(at, half), :]
                        (left_sent if k % 2 else left_kept)[k // 2, chip] = value[:, :columns]
                        (right_sent if k // 2 else right_kept)[k % 2, chip] = value[:, columns:]

    whole = lambda shape: pl.BlockSpec(shape, lambda i, order: (0,) * len(shape))
    sums = [
        jax.ShapeDtypeStruct((count, 2 * columns), jnp.float32),
        jax.ShapeDtypeStruct((count, 128), jnp.float32),
    ]
    part = jax.ShapeDtypeStruct((2, chips, half, columns), jnp.bfloat16)
    outs = [part] * 4 if last else sums
    scratch = [
        pltpu.VMEM((count, 2 * columns), jnp.bfloat16),
        *(pltpu.VMEM(value.shape, value.dtype) for value in sums),
    ]
    weights_spec = pl.BlockSpec((width, columns), lambda i, order: (owner_of(i, order), 0))
    return pl.pallas_call(
        body,
        out_shape=outs,
        grid_spec=pltpu.PrefetchScalarGridSpec(
            num_scalar_prefetch=1,
            grid=(4,),
            in_specs=[
                pl.BlockSpec((1, count, width), lambda i, order: (jnp.minimum(i, 1), 0, 0)),
                pl.BlockSpec((1, count, width), lambda i, order: (jnp.maximum(i - 2, 0), 0, 0)),
                whole(gains.shape),
                weights_spec,
                weights_spec,
            ]
            + [whole(value.shape) for value in so_far],
            out_specs=[whole(value.shape) for value in outs],
            scratch_shapes=scratch if last else [],
        ),
        compiler_params=pltpu.CompilerParams(vmem_limit_bytes=VMEM_BYTES),
        name="mix_channels",
    )(order, near, far, gains, own_proj, other_proj, *so_far)


def add_tokens(order, tokens, pieces, sizes):
    _, rows, quarters, _ = sizes
    half = rows // 2

    def body(order, tokens_ref, *refs):
        out_ref = refs[-1]
        columns = pieces[0].shape[2]
        core = order[quarters + 2]
        for at_core in range(2):

            @pl.when(core == at_core)
            def _():
                for place in range(len(pieces)):
                    part, k = place // quarters, place % quarters
                    at = pl.ds(pl.multiple_of(order[k] * rows + part * half, half), half)
                    for side in range(2):
                        start = (at_core if side == 0 else 1 - at_core) * columns
                        across = slice(start, start + columns)
                        out_ref[at, across] = (
                            tokens_ref[at, across].astype(jnp.float32)
                            + refs[place][side].astype(jnp.float32)
                        ).astype(jnp.bfloat16)

    whole = lambda value: pl.BlockSpec(value.shape, lambda i, order: (0,) * value.ndim)
    return pl.pallas_call(
        body,
        out_shape=jax.ShapeDtypeStruct(tokens.shape, tokens.dtype),
        grid_spec=pltpu.PrefetchScalarGridSpec(
            num_scalar_prefetch=1,
            grid=(1,),
            in_specs=[whole(tokens)] + [whole(value) for value in pieces],
            out_specs=whole(tokens),
        ),
        compiler_params=pltpu.CompilerParams(vmem_limit_bytes=VMEM_BYTES),
        name="add_tokens",
    )(order, tokens, *pieces)


VALUE_GROUPS = ((0,), (1, 2, 3))


def by_channel(
    tokens,
    norm_gain,
    gate_proj,
    value_proj,
    step_proj,
    state_proj,
    conv_value,
    conv_state,
    step_bias,
    decay_rate,
    skip_gain,
    mix_gain,
    out_proj,
    doc_lengths,
):
    stretches = lax.axis_size("seq")
    quarters = lax.axis_size("fsdp")
    chips = stretches // 2
    span, features = tokens.shape
    rows = span // quarters
    depth, inner_width = gate_proj.shape
    width = inner_width // stretches
    head_count = step_bias.shape[0]
    heads = head_count // stretches
    total_tokens = stretches * span
    sizes = (stretches, rows, quarters, width)
    seq_index = lax.axis_index("seq")
    fsdp_index = lax.axis_index("fsdp")
    chip, core = seq_index // 2, seq_index % 2
    where = jnp.stack([chip, core])
    order = jnp.stack(
        [fsdp_index ^ k for k in range(quarters)]
        + [(seq_index * heads).astype(jnp.int32), chip, core]
    )

    state_cols = lax.dynamic_index_in_dim(state_proj, fsdp_index, 1, keepdims=False)
    small = jnp.concatenate(
        [state_cols, step_proj, jnp.zeros((depth, 128 - head_count), jnp.bfloat16)], axis=1
    )
    starts = jnp.cumsum(doc_lengths) - doc_lengths
    index = jnp.arange(total_tokens, dtype=jnp.int32)[:, None]
    ages = jnp.min(
        jnp.where(starts[None, :] <= index, index - starts[None, :], total_tokens),
        axis=1,
        keepdims=True,
    )
    own_part = lambda value: lax.dynamic_slice_in_dim(value, seq_index * heads, heads, 0)
    lanes = lambda value: jnp.pad(own_part(value), (0, 128 - heads))[None, :]
    bias, rate = lanes(step_bias), lanes(decay_rate)
    skip = jnp.repeat(own_part(skip_gain), HEAD_DIM)[None, :]
    taps = lax.dynamic_slice_in_dim(conv_value, seq_index * width, width, 1)
    state_taps = lax.dynamic_index_in_dim(conv_state, fsdp_index, 1, keepdims=False)

    other_proj = swap_cores(out_proj)
    parts = lax.all_to_all(
        tokens.reshape(quarters, rows, features), "fsdp", split_axis=0, concat_axis=0, tiled=True
    )
    as_float = parts.astype(jnp.float32)
    mean_square = jnp.sum(as_float * as_float, axis=(0, 2), keepdims=True) / (
        quarters * features
    )
    normed = (
        as_float * lax.rsqrt(mean_square + EPSILON) * norm_gain.reshape(quarters, 1, features)
    ).astype(jnp.bfloat16)
    slices = (
        normed.reshape(quarters, rows, stretches // quarters, depth)
        .transpose(0, 2, 1, 3)
        .reshape(stretches, rows, depth)
    )
    own = lax.all_to_all(slices, "seq", split_axis=0, concat_axis=0, tiled=True).reshape(
        stretches * rows, depth
    )
    own, small, ages, bias, rate, skip, taps, state_taps, order, where = lax.optimization_barrier(
        (own, small, ages, bias, rate, skip, taps, state_taps, order, where)
    )

    near = [flip_fsdp(own, 1), flip_fsdp(own, 2)]
    near[0], near[1], again = lax.optimization_barrier((near[0], near[1], own))
    pieces = [own, *near, flip_fsdp(again, 3)]

    def reduced(inputs, *weights):
        lent, kept = share_partials(inputs, *weights, where, chips, width)
        return ring_reduce(kept, lent)

    ahead, behind = VALUE_GROUPS
    later = [pieces[k] for k in behind]
    first = reduced([pieces[k] for k in ahead], value_proj, gate_proj, small)
    second = reduced(later, value_proj, None, small)
    third = reduced(later, gate_proj, None, None)
    thin = []
    for members, trio in zip(VALUE_GROUPS, (first, second)):
        begin = len(members) * stretches * rows
        end = begin + len(members) * (rows + rows // 2)
        thin.append(
            add_up(trio[0][0, begin:end], trio[1][0, begin:end], trio[2][begin:end]).astype(
                jnp.bfloat16
            )
        )
    thin = jnp.concatenate(thin, axis=0)
    spread = [thin]
    for away in range(1, chips):
        spread.append(next_chip(thin, away))
    thin = jnp.stack(spread)
    thin_swapped = swap_cores(thin)
    outputs = scan_heads(
        order, (first, second), VALUE_GROUPS, thin, thin_swapped, ages, taps, state_taps,
        bias, rate, skip, sizes,
    )
    gate_start = len(ahead) * (stretches * rows + rows + rows // 2)
    parts = gate_outputs(
        order, outputs, (first, third), VALUE_GROUPS, (gate_start, 0), sizes
    )
    gains = mix_gain.reshape(stretches, width)
    ended = []
    for part in range(2):
        flat = lambda value: value.reshape(total_tokens // 4, width)
        came = swap_cores(parts[2 + part])
        blocks = [jnp.stack([flat(parts[part]), flat(came)])]
        for _ in range(1, chips):
            blocks.append(next_chip(blocks[-1]))
        so_far = mix_channels(
            order, *blocks[:2], 0, None, gains, out_proj, other_proj, sizes
        )
        left_kept, left_sent, right_kept, right_sent = mix_channels(
            order, *blocks[2:], 2, so_far, gains, out_proj, other_proj, sizes
        )
        left_got = flip_fsdp(left_sent, 1)
        right_got = flip_fsdp(right_sent, 2)
        left_sum = add_up(left_kept[1], left_got[1]).astype(jnp.bfloat16)
        right_sum = add_up(right_kept[1], right_got[1]).astype(jnp.bfloat16)
        left_more = flip_fsdp(left_sum, 2)
        right_more = flip_fsdp(right_sum, 1)
        summed = jnp.stack(
            [
                add_up(left_kept[0], left_got[0], left_more).astype(jnp.bfloat16),
                add_up(right_kept[0], right_got[0], right_more).astype(jnp.bfloat16),
            ],
            axis=1,
        )
        to_chip = lambda away: lax.dynamic_index_in_dim(summed, (chip + away) % chips, 0, False)
        arrived = [to_chip(0)]
        for away in range(1, chips):
            arrived.append(next_chip(to_chip(away), away))
        arrived = jnp.stack(arrived)
        from_chip = lambda other: lax.dynamic_index_in_dim(
            arrived, (chip + chips - other) % chips, 0, False
        )
        ended.append(from_chip(fsdp_index))
        for k in range(1, quarters):
            ended.append(flip_fsdp(from_chip(fsdp_index ^ k), k))
    return add_tokens(order, tokens, ended, sizes)


def layer(*arguments):
    stretches, quarters = lax.axis_size("seq"), lax.axis_size("fsdp")
    span, inner_width = arguments[0].shape[0], arguments[2].shape[1]
    heads = arguments[8].shape[0]
    width = inner_width // stretches
    aligned = (
        quarters == G
        and quarters == 4
        and stretches == 2 * quarters
        and width == 2 * N
        and width % HEAD_DIM == 0
        and heads <= 128
        and span % (16 * quarters) == 0
        and span % 128 == 0
    )
    return (by_channel if aligned else by_stretch)(*arguments)


def solution(mesh):
    return jax.shard_map(
        layer,
        mesh=mesh,
        in_specs=(
            P("seq", "fsdp"),
            P(),
            P("seq", "fsdp"),
            P("seq", "fsdp"),
            P("seq", "fsdp"),
            P("seq", None, None),
            P(None, "fsdp"),
            P(),
            P("fsdp"),
            P("fsdp"),
            P("fsdp"),
            P("fsdp"),
            P("fsdp", "seq"),
            P(),
        ),
        out_specs=P("seq", "fsdp"),
        check_vma=False,
    )
```

```python
import jax
import jax.numpy as jnp
from jax import lax
from jax.experimental import pallas as pl
from jax.experimental.pallas import tpu as pltpu
from jax.sharding import PartitionSpec as P

H = 128
HEAD_DIM = 64
N = 128
G = 4


EPSILON = 1e-05
PRECISE = lax.Precision.HIGHEST


def from_behind(value, axis, steps):
    count = lax.axis_size(axis)
    leading, last = (max(0, -steps), min(count, count - steps))
    return lax.ppermute(value, axis, [(source, source + steps) for source in range(leading, last)])


def partner(block, axis, distance):
    count = lax.axis_size(axis)
    route = []
    for low in range(count):
        high = low | 1 << distance
        if high != low and high < count:
            route += [(low, high), (high, low)]
    return lax.ppermute(block, axis, route)


def by_stretch(
    tokens,
    norm_gain,
    gate_proj,
    value_proj,
    step_proj,
    state_proj,
    conv_value,
    conv_state,
    step_bias,
    decay_rate,
    skip_gain,
    mix_gain,
    out_proj,
    doc_lengths,
):
    span_rows = tokens.shape[0]
    seq_index = lax.axis_index("seq")
    fsdp_index = lax.axis_index("fsdp")
    head_count = step_bias.shape[0]
    inner_width = gate_proj.shape[1]
    group_devices = lax.axis_size("fsdp") // G
    group_index = fsdp_index // group_devices
    gathered = lax.all_gather(tokens, "fsdp", axis=1, tiled=True)
    as_float = gathered.astype(jnp.float32)
    normed = (
        as_float
        * lax.rsqrt(jnp.mean(as_float * as_float, axis=1, keepdims=True) + EPSILON)
        * norm_gain
    ).astype(jnp.bfloat16)
    state_cols = lax.dynamic_index_in_dim(state_proj, group_index, 1, keepdims=False)
    stacked = jnp.concatenate([gate_proj, value_proj, state_cols, step_proj], axis=1)
    spread = lax.all_to_all(normed, "seq", split_axis=1, concat_axis=0, tiled=True)
    summed = lax.psum_scatter(
        jnp.dot(spread, stacked, preferred_element_type=jnp.float32),
        "seq",
        scatter_dimension=0,
        tiled=True,
    )
    gate = summed[:, :inner_width]
    values = summed[:, inner_width : 2 * inner_width]
    states = summed[:, 2 * inner_width : 2 * inner_width + 2 * N]
    raw_step = summed[:, 2 * inner_width + 2 * N :]
    raw_mix = jnp.concatenate([values, states], axis=1).astype(jnp.bfloat16)
    tail_rows = from_behind(raw_mix[span_rows - 3 :], "seq", 1)
    extended = jnp.concatenate([tail_rows, raw_mix], axis=0)
    starts = jnp.cumsum(doc_lengths) - doc_lengths
    span_start = seq_index * span_rows
    positions = span_start - 3 + jnp.arange(span_rows + 3, dtype=jnp.int32)
    segment_ext = jnp.sum(starts[None, :] <= positions[:, None], axis=1) - 1
    segment = segment_ext[3:]
    taps = jnp.concatenate(
        [conv_value, lax.dynamic_index_in_dim(conv_state, group_index, 1, keepdims=False)], axis=1
    )
    convolved = jnp.zeros((span_rows, taps.shape[1]), jnp.float32)
    for offset in range(4):
        same_doc = segment_ext[offset : offset + span_rows] == segment
        convolved = (
            convolved
            + jnp.where(
                same_doc[:, None], extended[offset : offset + span_rows].astype(jnp.float32), 0.0
            )
            * taps[offset]
        )
    rounded = lax.optimization_barrier(jax.nn.silu(convolved).astype(jnp.bfloat16))
    activated = rounded.astype(jnp.float32)
    inputs = activated[:, :inner_width].reshape(span_rows, head_count, HEAD_DIM)
    in_map = activated[:, inner_width : inner_width + N]
    out_map = activated[:, inner_width + N :]
    in_half = rounded[:, inner_width : inner_width + N]
    out_half = rounded[:, inner_width + N :]
    step_size = jax.nn.softplus(raw_step + step_bias)
    log_decay = -decay_rate * step_size
    cumulative = jnp.cumsum(log_decay, axis=0)
    order = jnp.arange(span_rows)
    causal = (segment[:, None] == segment[None, :]) & (order[:, None] >= order[None, :])
    gaps = cumulative.T[:, :, None] - cumulative.T[:, None, :]
    decay = jnp.exp(jnp.where(causal[None], gaps, -jnp.inf))
    scores = jnp.dot(out_half, in_half.T, preferred_element_type=jnp.float32)
    mixing = decay * scores[None] * step_size.T[:, None, :]
    intra = jnp.einsum("hts,shp->thp", mixing, inputs, precision=PRECISE)
    last_segment = segment[span_rows - 1]
    prior_segment = segment_ext[2]
    in_last = segment == last_segment
    to_end = (
        jnp.where(in_last[:, None], jnp.exp(cumulative[span_rows - 1][None, :] - cumulative), 0.0)
        * step_size
    )
    local_state = jnp.einsum("sh,shp,sn->hpn", to_end, inputs, in_map, precision=PRECISE)
    passing = jnp.where(last_segment == prior_segment, jnp.exp(cumulative[span_rows - 1]), 0.0)
    empty = jnp.zeros_like(local_state)

    def relay(turn, incoming):
        return from_behind(
            (passing[:, None, None] * incoming + local_state).astype(jnp.bfloat16), "seq", 1
        ).astype(jnp.float32)

    incoming = lax.fori_loop(0, lax.axis_size("seq") - 1, relay, empty)
    carried = jnp.where((segment == prior_segment)[:, None], jnp.exp(cumulative), 0.0)
    from_state = (
        jnp.einsum("tn,hpn->thp", out_map, incoming, precision=PRECISE) * carried[:, :, None]
    )
    outputs = intra + from_state + skip_gain[None, :, None] * inputs
    gated = outputs.reshape(span_rows, inner_width) * jax.nn.silu(gate)
    squares = jnp.sum(gated * gated, axis=1)
    for bit in range(group_devices.bit_length() - 1):
        squares = squares + partner(squares, "fsdp", bit)
    scaled = (
        gated * lax.rsqrt(squares[:, None] / (H * HEAD_DIM // G) + EPSILON) * mix_gain
    ).astype(jnp.bfloat16)
    terms = jnp.dot(
        scaled,
        lax.all_gather(out_proj, "seq", axis=1, tiled=True),
        preferred_element_type=jnp.float32,
    )
    mixed = lax.psum_scatter(
        terms.astype(jnp.bfloat16), "fsdp", scatter_dimension=1, tiled=True
    ).astype(jnp.float32)
    return (tokens.astype(jnp.float32) + mixed).astype(jnp.bfloat16)


VMEM_BYTES = 20 << 20
SCAN_BYTES = 56 << 20
FIRST_BYTES = 56 << 20


def swap_cores(value):
    count = lax.axis_size("seq")
    return lax.ppermute(value, "seq", [(place, place ^ 1) for place in range(count)])


def next_chip(value, away=1):
    count = lax.axis_size("seq")
    route = [(place, (place + 2 * away) % count) for place in range(count)]
    return lax.ppermute(value, "seq", route)


def flip_fsdp(value, bits):
    count = lax.axis_size("fsdp")
    return lax.ppermute(value, "fsdp", [(place, place ^ bits) for place in range(count)])


def share_partials(pieces, projections, plan, small, thin_places, where, chips, width, grant):
    depth, count = pieces[0].shape[1], pieces[0].shape[0]
    rows = count // (2 * chips)
    number = len(pieces)
    thin_start = len(plan) * count
    thins = len(thin_places)
    thin_inputs = [small] if thins else []
    maps_width = small.shape[1] - 128
    total_rows = thin_start + thins * (rows + rows // 2)

    def body(where, *refs):
        row_refs, refs = refs[:number], refs[number:]
        weight_refs, refs = refs[: len(projections)], refs[len(projections) :]
        lent_ref, kept_ref, thin = refs[-3:]
        index, core = pl.program_id(0), where[1]
        chip = lax.rem(where[0] + chips - index, chips)
        first = core == 0

        if thins:

            @pl.when(index == 0)
            def _():
                for place, piece in enumerate(thin_places):
                    thin[place * count : (place + 1) * count] = jnp.dot(
                        row_refs[piece][...], refs[0][...], preferred_element_type=jnp.float32
                    ).astype(jnp.bfloat16)

            for out_ref, own in ((lent_ref, 1 - core), (kept_ref, core)):
                for place in range(thins):
                    at = place * count + (own * chips + chip) * rows
                    to = thin_start + place * rows
                    out_ref[0, to : to + rows] = thin[
                        pl.ds(pl.multiple_of(at, rows), rows), :maps_width
                    ]
                    to = thin_start + thins * rows + place * rows // 2
                    halves = [
                        thin[
                            pl.ds(pl.multiple_of(at + part * rows // 2, rows // 2), rows // 2),
                            maps_width:,
                        ]
                        for part in range(2)
                    ]
                    out_ref[0, to : to + rows // 2] = jnp.concatenate(halves, axis=1)

        for place, (which, piece) in enumerate(plan):
            both = jnp.dot(
                row_refs[piece][...], weight_refs[which][...], preferred_element_type=jnp.float32
            ).astype(jnp.bfloat16)
            at = slice(place * count, (place + 1) * count)
            kept_ref[0, at] = jnp.where(first, both[:, :width], both[:, width:])
            lent_ref[0, at] = jnp.where(first, both[:, width:], both[:, :width])

    out = jax.ShapeDtypeStruct((chips, total_rows, width), jnp.bfloat16)
    return pl.pallas_call(
        body,
        out_shape=[out, out],
        grid_spec=pltpu.PrefetchScalarGridSpec(
            num_scalar_prefetch=1,
            grid=(chips,),
            in_specs=[pl.BlockSpec((count, depth), lambda i, where: (0, 0)) for _ in pieces]
            + [
                pl.BlockSpec(
                    (depth, 2 * width), lambda i, where: (0, lax.rem(where[0] + chips - i, chips))
                )
                for _ in projections
            ]
            + [pl.BlockSpec(value.shape, lambda i, where: (0, 0)) for value in thin_inputs],
            out_specs=[pl.BlockSpec((1, total_rows, width), lambda i, where: (i, 0, 0))] * 2,
            scratch_shapes=[pltpu.VMEM((max(1, thins) * count, maps_width + 128), jnp.bfloat16)],
        ),
        compiler_params=pltpu.CompilerParams(vmem_limit_bytes=grant),
        name="share_partials",
    )(where, *pieces, *projections, *thin_inputs)


def add_up(*terms):
    total = terms[0].astype(jnp.float32)
    for term in terms[1:]:
        total = total + term.astype(jnp.float32)
    return total


def ring_reduce(kept, lent):
    got = swap_cores(lent)
    chips = kept.shape[0]
    passed = []
    for step in range(1, chips):
        sent = add_up(kept[step], got[step], *passed).astype(jnp.bfloat16)
        passed = [next_chip(sent)]
    return kept, got, passed[0]


def scan_heads(order, trios, groups, thin_groups, thin, thin_swapped, starts, taps, state_taps, bias, rate, skip, sizes):
    stretches, rows, quarters, width = sizes
    span = rows * quarters
    tokens = stretches * span
    count = stretches * rows
    half = rows // 2
    chips = stretches // 2
    heads = width // HEAD_DIM
    flat = [value for trio in trios for value in trio]
    number = len(flat)

    def body(order, starts_ref, *refs):
        trio_refs, refs = refs[:number], refs[number:]
        thin_ref, swapped_ref, taps_ref, state_taps_ref, bias_ref = refs[:5]
        rate_ref, skip_ref, out_ref, values, maps, steps, state, ages = refs[5:]
        token = lax.broadcasted_iota(jnp.int32, (stretches, span), 0) * span
        token = token + lax.broadcasted_iota(jnp.int32, (stretches, span), 1)
        age_rows = jnp.full((stretches, span), tokens, jnp.int32)
        for document in range(starts.shape[0]):
            since = token - starts_ref[document]
            age_rows = jnp.where(since >= 0, jnp.minimum(age_rows, since), age_rows)
        ages[...] = age_rows.astype(jnp.float32)
        first_head, chip, core = (order[quarters + place] for place in range(3))
        values[:8] = jnp.zeros((8, width), jnp.float32)
        maps[:8] = jnp.zeros((8, 2 * N), jnp.float32)

        def place_rows(stretch, carry):
            for group, members in enumerate(groups):
                kept, got, last = trio_refs[3 * group : 3 * group + 3]
                for place, k in enumerate(members):
                    at = pl.multiple_of(place * count + stretch * rows, rows)
                    to = pl.multiple_of(stretch * span + order[k] * rows, rows)
                    total = (
                        kept[0, pl.ds(at, rows), :].astype(jnp.float32)
                        + got[0, pl.ds(at, rows), :].astype(jnp.float32)
                        + last[pl.ds(at, rows), :].astype(jnp.float32)
                    )
                    values[pl.ds(to + 8, rows), :] = total.astype(jnp.bfloat16).astype(
                        jnp.float32
                    )
            return carry

        lax.fori_loop(0, stretches, place_rows, 0)
        for source, own_core in ((thin_ref, core), (swapped_ref, 1 - core)):
            for away in range(chips):
                stretch = own_core * chips + lax.rem(chip + chips - away, chips)
                base = 0
                for members in thin_groups:
                    for place, k in enumerate(members):
                        to = pl.multiple_of(stretch * span + order[k] * rows, rows)
                        at = base + place * rows
                        maps[pl.ds(to + 8, rows), :] = source[away, at : at + rows].astype(
                            jnp.float32
                        )
                        at = base + len(members) * rows + place * half
                        for part in range(2):
                            steps[pl.ds(pl.multiple_of(to + part * half, half), half), :] = source[
                                away, at : at + half, part * 128 : (part + 1) * 128
                            ].astype(jnp.float32)
                    base += len(members) * (rows + half)
        state[...] = jnp.zeros_like(state)
        row = lax.broadcasted_iota(jnp.int32, (span, span), 0)
        gap = row - lax.broadcasted_iota(jnp.int32, (span, span), 1)
        lower = jnp.where(gap >= 0, 1.0, 0.0)
        here = lax.broadcasted_iota(jnp.int32, (span, 1), 0)
        head_of = lax.broadcasted_iota(jnp.int32, (1, width), 1) // HEAD_DIM

        def by_head(columns):
            wide = jnp.broadcast_to(columns[:, 0:1], (columns.shape[0], width))
            for head in range(1, heads):
                wide = jnp.where(head_of == head, columns[:, head : head + 1], wide)
            return wide

        def convolve(source, gains, start, age):
            block = source[pl.ds(start, span + 8), :]
            total = block[8:] * gains[3:4]
            for lag in range(1, 4):
                total = total + jnp.where(age >= lag, block[8 - lag : 8 - lag + span], 0.0) * gains[
                    3 - lag : 4 - lag
                ]
            return (total * jax.nn.sigmoid(total)).astype(jnp.bfloat16)

        def chunk(index, carry):
            start = pl.multiple_of(index * span, span)
            age = jnp.broadcast_to(ages[pl.ds(index, 1), :], (span, span)).T.astype(jnp.int32)
            age = age[:, :1]
            last_age = age[span - 1 :]
            inputs = convolve(values, taps_ref[...], start, age)
            both = convolve(maps, state_taps_ref[...], start, age)
            in_map, out_map = both[:, :N], both[:, N:]
            raw = pltpu.roll(steps[pl.ds(start, span), :], lax.rem(128 - first_head, 128), 1)
            raw = raw + bias_ref[...]
            size = jnp.maximum(raw, 0.0) + jnp.log1p(jnp.exp(-jnp.abs(raw)))
            total = jnp.dot(
                lower,
                -rate_ref[...] * size,
                precision=PRECISE,
                preferred_element_type=jnp.float32,
            )
            total_rows, size_rows = total.T, size.T
            scores = lax.dot_general(
                out_map, in_map, (((1,), (1,)), ((), ())), preferred_element_type=jnp.float32
            )
            near = (gap >= 0) & (gap <= age)
            history = jnp.zeros((span, width), jnp.float32)
            for head in range(heads):
                decay = jnp.exp(
                    jnp.where(
                        near, total[:, head : head + 1] - total_rows[head : head + 1], -jnp.inf
                    )
                )
                mixing = (decay * scores * size_rows[head : head + 1]).astype(jnp.bfloat16)
                part = jnp.dot(mixing, inputs, preferred_element_type=jnp.float32)
                history = jnp.where(head_of == head, part, history)
            old = state[...]
            carried = by_head(jnp.where(age > here, jnp.exp(total), 0.0))
            history = history + carried * jnp.dot(
                out_map, old.astype(jnp.bfloat16), preferred_element_type=jnp.float32
            )
            wide = inputs.astype(jnp.float32)
            out_ref[pl.ds(start, span), :] = history + skip_ref[...] * wide
            end = total[span - 1 :]
            to_end = by_head(
                jnp.where(span - 1 - here <= last_age, jnp.exp(end - total), 0.0) * size
            )
            keep = by_head(jnp.where(last_age >= span, jnp.exp(end), 0.0))
            state[...] = keep * old + lax.dot_general(
                in_map,
                (wide * to_end).astype(jnp.bfloat16),
                (((0,), (0,)), ((), ())),
                preferred_element_type=jnp.float32,
            )
            return carry

        lax.fori_loop(0, stretches, chunk, 0)

    whole = lambda value: pl.BlockSpec(value.shape, lambda i, order, starts: (0,) * value.ndim)
    trio_specs = [
        pl.BlockSpec((1,) + value.shape[1:], lambda i, order, starts: (0, 0, 0))
        if value.ndim == 3
        else whole(value)
        for value in flat
    ]
    rest = (thin, thin_swapped, taps, state_taps, bias, rate, skip)
    return pl.pallas_call(
        body,
        out_shape=jax.ShapeDtypeStruct((tokens, width), jnp.float32),
        grid_spec=pltpu.PrefetchScalarGridSpec(
            num_scalar_prefetch=2,
            grid=(1,),
            in_specs=trio_specs + [whole(value) for value in rest],
            out_specs=pl.BlockSpec((tokens, width), lambda i, order, starts: (0, 0)),
            scratch_shapes=[
                pltpu.VMEM((tokens + 8, width), jnp.float32),
                pltpu.VMEM((tokens + 8, 2 * N), jnp.float32),
                pltpu.VMEM((tokens, 128), jnp.float32),
                pltpu.VMEM((N, width), jnp.float32),
                pltpu.VMEM((stretches, span), jnp.float32),
            ],
        ),
        compiler_params=pltpu.CompilerParams(vmem_limit_bytes=SCAN_BYTES),
        name="scan_heads",
    )(order, starts, *flat, *rest)


def gate_outputs(order, outputs, trios, groups, offsets, sizes):
    stretches, rows, quarters, width = sizes
    count, half, chips = stretches * rows, rows // 2, stretches // 2
    flat = [value for trio in trios for value in trio]
    number = len(flat)

    def body(order, *refs):
        trio_refs, outputs_ref, parts = refs[:number], refs[number], refs[number + 1 :]
        core = order[quarters + 2]

        def one_chip(chip, carry):
            for role, stretch in enumerate((2 * chip + core, 2 * chip + 1 - core)):
                for group, members in enumerate(groups):
                    kept, got, last = trio_refs[3 * group : 3 * group + 3]
                    for place, k in enumerate(members):
                        at = offsets[group] + place * count + stretch * rows
                        at = pl.ds(pl.multiple_of(at, 16), rows)
                        gate = (
                            kept[0, at, :].astype(jnp.float32)
                            + got[0, at, :].astype(jnp.float32)
                            + last[at, :].astype(jnp.float32)
                        )
                        value = (
                            outputs_ref[stretch, order[k]] * gate * jax.nn.sigmoid(gate)
                        ).astype(jnp.bfloat16)
                        for part in range(2):
                            parts[2 * role + part][chip, order[k]] = value[
                                part * half : (part + 1) * half
                            ]
            return carry

        lax.fori_loop(0, chips, one_chip, 0)

    whole = lambda shape: pl.BlockSpec(shape, lambda i, order: (0,) * len(shape))
    shape = (chips, quarters, half, width)
    return pl.pallas_call(
        body,
        out_shape=[jax.ShapeDtypeStruct(shape, jnp.bfloat16)] * 4,
        grid_spec=pltpu.PrefetchScalarGridSpec(
            num_scalar_prefetch=1,
            grid=(1,),
            in_specs=[
                whole((1,) + value.shape[1:] if value.ndim == 3 else value.shape)
                for value in flat
            ]
            + [whole((stretches, quarters, rows, width))],
            out_specs=[whole(shape)] * 4,
        ),
        compiler_params=pltpu.CompilerParams(vmem_limit_bytes=SCAN_BYTES),
        name="gate_outputs",
    )(order, *flat, outputs.reshape(stretches, quarters, rows, width))


def mix_channels(order, pairs, away, so_far, gains, own_proj, other_proj, sizes):
    stretches, rows, quarters, width = sizes
    half, chips = rows // 2, stretches // 2
    count = pairs[0].shape[1]
    number = len(pairs) // 2
    channels, columns = own_proj.shape
    last = so_far is not None
    so_far = list(so_far) if last else []

    def owner_of(i, order):
        chip, core = order[quarters + 1], order[quarters + 2]
        return 2 * lax.rem(chip + chips - away - i // 2, chips) + lax.rem(core + i, 2)

    def body(order, *refs):
        pair_refs, refs = refs[: len(pairs)], refs[len(pairs) :]
        gains_ref, own_ref, other_ref, refs = *refs[:3], refs[3:]
        before, refs = refs[: len(so_far)], refs[len(so_far) :]
        totals = refs[5:] if last else refs
        index = pl.program_id(0)

        @pl.when(index == 0)
        def _():
            for place, total in enumerate(totals):
                total[...] = before[place][...] if last else jnp.zeros_like(total)

        for part in range(number):
            near_ref, far_ref = pair_refs[2 * part : 2 * part + 2]
            total, squares = totals[2 * part : 2 * part + 2]
            block = jnp.where(index < 2, near_ref[0], far_ref[0]).astype(jnp.float32)
            squares[...] += jnp.broadcast_to(
                jnp.sum(block * block, axis=1, keepdims=True), squares.shape
            )
            gain = gains_ref[pl.ds(owner_of(index, order), 1), :]
            gained = (block * gain).astype(jnp.bfloat16)
            for side, weights_ref in enumerate((own_ref, other_ref)):
                total[:, side * columns : (side + 1) * columns] += jnp.dot(
                    gained, weights_ref[...], preferred_element_type=jnp.float32
                )
        if last:
            total, squares, rounded = *totals, refs[4]

            @pl.when(index == pl.num_programs(0) - 1)
            def _():
                factor = lax.rsqrt(squares[:, :1] / channels + EPSILON)
                rounded[...] = (total[...] * factor).astype(jnp.bfloat16)
                left_kept, left_sent, right_kept, right_sent = refs[:4]
                for k in range(4):
                    for away in range(chips):
                        goal = lax.rem(order[quarters + 1] + away, chips)
                        at = pl.multiple_of((goal * quarters + order[k]) * half, half)
                        value = rounded[pl.ds(at, half), :]
                        (left_sent if k % 2 else left_kept)[k // 2, away] = value[:, :columns]
                        (right_sent if k // 2 else right_kept)[k % 2, away] = value[:, columns:]

    whole = lambda shape: pl.BlockSpec(shape, lambda i, order: (0,) * len(shape))
    sums = [
        jax.ShapeDtypeStruct((count, 2 * columns), jnp.float32),
        jax.ShapeDtypeStruct((count, 128), jnp.float32),
    ] * number
    part = jax.ShapeDtypeStruct((2, chips, half, columns), jnp.bfloat16)
    outs = [part] * 4 if last else sums
    scratch = [
        pltpu.VMEM((count, 2 * columns), jnp.bfloat16),
        *(pltpu.VMEM(value.shape, value.dtype) for value in sums),
    ]
    weights_spec = pl.BlockSpec((width, columns), lambda i, order: (owner_of(i, order), 0))
    pair_specs = [
        pl.BlockSpec((1, count, width), lambda i, order: (jnp.minimum(i, 1), 0, 0)),
        pl.BlockSpec((1, count, width), lambda i, order: (jnp.maximum(i - 2, 0), 0, 0)),
    ]
    return pl.pallas_call(
        body,
        out_shape=outs,
        grid_spec=pltpu.PrefetchScalarGridSpec(
            num_scalar_prefetch=1,
            grid=(4,),
            in_specs=pair_specs * number
            + [whole(gains.shape), weights_spec, weights_spec]
            + [whole(value.shape) for value in so_far],
            out_specs=[whole(value.shape) for value in outs],
            scratch_shapes=scratch if last else [],
        ),
        compiler_params=pltpu.CompilerParams(vmem_limit_bytes=VMEM_BYTES),
        name="mix_channels",
    )(order, *pairs, gains, own_proj, other_proj, *so_far)


def add_tokens(order, tokens, pieces, sizes):
    _, rows, quarters, _ = sizes
    half = rows // 2

    def body(order, tokens_ref, *refs):
        out_ref = refs[-1]
        columns = pieces[0].shape[2]
        core = order[quarters + 2]
        for at_core in range(2):

            @pl.when(core == at_core)
            def _():
                for part, k in ((part, k) for part in range(2) for k in range(quarters)):
                    at = pl.ds(pl.multiple_of(order[k] * rows + part * half, half), half)
                    for side in range(2):
                        start = (at_core if side == 0 else 1 - at_core) * columns
                        across = slice(start, start + columns)
                        out_ref[at, across] = (
                            tokens_ref[at, across].astype(jnp.float32)
                            + refs[k][2 * part + side].astype(jnp.float32)
                        ).astype(jnp.bfloat16)

    whole = lambda value: pl.BlockSpec(value.shape, lambda i, order: (0,) * value.ndim)
    return pl.pallas_call(
        body,
        out_shape=jax.ShapeDtypeStruct(tokens.shape, tokens.dtype),
        grid_spec=pltpu.PrefetchScalarGridSpec(
            num_scalar_prefetch=1,
            grid=(1,),
            in_specs=[whole(tokens)] + [whole(value) for value in pieces],
            out_specs=whole(tokens),
        ),
        compiler_params=pltpu.CompilerParams(vmem_limit_bytes=VMEM_BYTES),
        name="add_tokens",
    )(order, tokens, *pieces)


def by_channel(
    tokens,
    norm_gain,
    gate_proj,
    value_proj,
    step_proj,
    state_proj,
    conv_value,
    conv_state,
    step_bias,
    decay_rate,
    skip_gain,
    mix_gain,
    out_proj,
    doc_lengths,
):
    stretches = lax.axis_size("seq")
    quarters = lax.axis_size("fsdp")
    chips = stretches // 2
    span, features = tokens.shape
    rows = span // quarters
    depth, inner_width = gate_proj.shape
    width = inner_width // stretches
    head_count = step_bias.shape[0]
    heads = head_count // stretches
    total_tokens = stretches * span
    sizes = (stretches, rows, quarters, width)
    seq_index = lax.axis_index("seq")
    fsdp_index = lax.axis_index("fsdp")
    chip, core = seq_index // 2, seq_index % 2
    where = jnp.stack([chip, core])
    order = jnp.stack(
        [fsdp_index ^ k for k in range(quarters)]
        + [(seq_index * heads).astype(jnp.int32), chip, core]
    )

    state_cols = lax.dynamic_index_in_dim(state_proj, fsdp_index, 1, keepdims=False)
    small = jnp.concatenate(
        [state_cols, step_proj, jnp.zeros((depth, 128 - head_count), jnp.bfloat16)], axis=1
    )
    starts = (jnp.cumsum(doc_lengths) - doc_lengths).astype(jnp.int32)
    own_part = lambda value: lax.dynamic_slice_in_dim(value, seq_index * heads, heads, 0)
    lanes = lambda value: jnp.pad(own_part(value), (0, 128 - heads))[None, :]
    bias, rate = lanes(step_bias), lanes(decay_rate)
    skip = jnp.repeat(own_part(skip_gain), HEAD_DIM)[None, :]
    taps = lax.dynamic_slice_in_dim(conv_value, seq_index * width, width, 1)
    state_taps = lax.dynamic_index_in_dim(conv_state, fsdp_index, 1, keepdims=False)

    other_proj = swap_cores(out_proj)
    parts = lax.all_to_all(
        tokens.reshape(quarters, rows, features), "fsdp", split_axis=0, concat_axis=0, tiled=True
    )
    as_float = parts.astype(jnp.float32)
    mean_square = jnp.sum(as_float * as_float, axis=(0, 2), keepdims=True) / (
        quarters * features
    )
    normed = (
        as_float * lax.rsqrt(mean_square + EPSILON) * norm_gain.reshape(quarters, 1, features)
    ).astype(jnp.bfloat16)
    slices = (
        normed.reshape(quarters, rows, stretches // quarters, depth)
        .transpose(0, 2, 1, 3)
        .reshape(stretches, rows, depth)
    )
    own = lax.all_to_all(slices, "seq", split_axis=0, concat_axis=0, tiled=True).reshape(
        stretches * rows, depth
    )
    own, small, starts, bias, rate, skip, taps, state_taps, order, where = lax.optimization_barrier(
        (own, small, starts, bias, rate, skip, taps, state_taps, order, where)
    )

    near = [flip_fsdp(own, 1), flip_fsdp(own, 2)]
    near[0], near[1], again = lax.optimization_barrier((near[0], near[1], own))
    pieces = [own, *near, flip_fsdp(again, 3)]

    def reduced(members, projections, plan, thin_places=(), grant=VMEM_BYTES):
        lent, kept = share_partials(
            [pieces[k] for k in members], projections, plan, small, thin_places, where,
            chips, width, grant,
        )
        return ring_reduce(kept, lent)

    count = stretches * rows
    first = reduced((0,), [value_proj, gate_proj], ((0, 0), (1, 0)), (0,), FIRST_BYTES)
    second = reduced((3, 1, 2), [value_proj], ((0, 0),), (0, 1, 2))
    third = reduced((1, 2), [value_proj], ((0, 0), (0, 1)))
    fourth = reduced((1, 2, 3), [gate_proj], ((0, 0), (0, 1), (0, 2)))
    value_groups, thin_groups = ((0,), (3,), (1, 2)), ((0,), (3, 1, 2))
    gate_groups, gate_starts = ((0,), (1, 2, 3)), (count, 0)
    thin = jnp.concatenate(
        [
            add_up(trio[0][0, start:], trio[1][0, start:], trio[2][start:]).astype(
                jnp.bfloat16
            )
            for trio, start in ((first, 2 * count), (second, count))
        ]
    )
    spread = [thin]
    for _ in range(1, chips):
        spread.append(next_chip(spread[-1]))
    thin = jnp.stack(spread)
    thin_swapped = swap_cores(thin)
    outputs = scan_heads(
        order, (first, second, third), value_groups, thin_groups, thin, thin_swapped, starts, taps, state_taps,
        bias, rate, skip, sizes,
    )
    parts = gate_outputs(order, outputs, (first, fourth), gate_groups, gate_starts, sizes)
    gains = mix_gain.reshape(stretches, width)
    sums, shares = [], []
    for part in range(2):
        flat = lambda value: value.reshape(total_tokens // 4, width)
        came = swap_cores(parts[2 + part])
        blocks = [jnp.stack([flat(parts[part]), flat(came)])]
        for _ in range(1, chips):
            blocks.append(next_chip(blocks[-1]))
        shares.append(blocks)
    so_far = mix_channels(
        order, shares[0][:2] + shares[1][:2], 0, None, gains, out_proj, other_proj, sizes
    )
    for part in range(2):
        left_kept, left_sent, right_kept, right_sent = mix_channels(
            order, shares[part][2:], 2, so_far[2 * part : 2 * part + 2], gains, out_proj,
            other_proj, sizes,
        )
        left_got = flip_fsdp(left_sent, 1)
        right_got = flip_fsdp(right_sent, 2)
        left_sum = add_up(left_kept[1], left_got[1]).astype(jnp.bfloat16)
        right_sum = add_up(right_kept[1], right_got[1]).astype(jnp.bfloat16)
        left_more = flip_fsdp(left_sum, 2)
        right_more = flip_fsdp(right_sum, 1)
        sums.append((left_kept[0], left_got[0], left_more, right_kept[0], right_got[0], right_more))

    def to_chip(away):
        pick = lambda terms: add_up(*(term[away] for term in terms)).astype(jnp.bfloat16)
        return jnp.stack([pick(terms[side : side + 3]) for terms in sums for side in (0, 3)])

    arrived = [to_chip(0)]
    for away in range(1, chips):
        arrived.append(next_chip(to_chip(away), away))

    def from_chip(other):
        back = (chip + chips - other) % chips
        value = arrived[0]
        for away in range(1, chips):
            value = jnp.where(back == away, arrived[away], value)
        return value

    ended = [from_chip(fsdp_index)]
    for k in range(1, quarters):
        ended.append(flip_fsdp(from_chip(fsdp_index ^ k), k))
    return add_tokens(order, tokens, ended, sizes)


def layer(*arguments):
    stretches, quarters = lax.axis_size("seq"), lax.axis_size("fsdp")
    span, inner_width = arguments[0].shape[0], arguments[2].shape[1]
    heads = arguments[8].shape[0]
    width = inner_width // stretches
    aligned = (
        quarters == G
        and quarters == 4
        and stretches == 2 * quarters
        and width == 2 * N
        and width % HEAD_DIM == 0
        and heads <= 128
        and span % (16 * quarters) == 0
        and span % 128 == 0
    )
    return (by_channel if aligned else by_stretch)(*arguments)


def solution(mesh):
    return jax.shard_map(
        layer,
        mesh=mesh,
        in_specs=(
            P("seq", "fsdp"),
            P(),
            P("seq", "fsdp"),
            P("seq", "fsdp"),
            P("seq", "fsdp"),
            P("seq", None, None),
            P(None, "fsdp"),
            P(),
            P("fsdp"),
            P("fsdp"),
            P("fsdp"),
            P("fsdp"),
            P("fsdp", "seq"),
            P(),
        ),
        out_specs=P("seq", "fsdp"),
        check_vma=False,
    )
```

```python
import jax
import jax.numpy as jnp
from jax import lax
from jax.experimental import pallas as pl
from jax.experimental.pallas import tpu as pltpu
from jax.sharding import PartitionSpec as P

H = 128
HEAD_DIM = 64
N = 128
G = 4


EPSILON = 1e-05
PRECISE = lax.Precision.HIGHEST


def from_behind(value, axis, steps):
    count = lax.axis_size(axis)
    leading, last = (max(0, -steps), min(count, count - steps))
    return lax.ppermute(value, axis, [(source, source + steps) for source in range(leading, last)])


def partner(block, axis, distance):
    count = lax.axis_size(axis)
    route = []
    for low in range(count):
        high = low | 1 << distance
        if high != low and high < count:
            route += [(low, high), (high, low)]
    return lax.ppermute(block, axis, route)


def by_stretch(
    tokens,
    norm_gain,
    gate_proj,
    value_proj,
    step_proj,
    state_proj,
    conv_value,
    conv_state,
    step_bias,
    decay_rate,
    skip_gain,
    mix_gain,
    out_proj,
    doc_lengths,
):
    span_rows = tokens.shape[0]
    seq_index = lax.axis_index("seq")
    fsdp_index = lax.axis_index("fsdp")
    head_count = step_bias.shape[0]
    inner_width = gate_proj.shape[1]
    group_devices = lax.axis_size("fsdp") // G
    group_index = fsdp_index // group_devices
    gathered = lax.all_gather(tokens, "fsdp", axis=1, tiled=True)
    as_float = gathered.astype(jnp.float32)
    normed = (
        as_float
        * lax.rsqrt(jnp.mean(as_float * as_float, axis=1, keepdims=True) + EPSILON)
        * norm_gain
    ).astype(jnp.bfloat16)
    state_cols = lax.dynamic_index_in_dim(state_proj, group_index, 1, keepdims=False)
    stacked = jnp.concatenate([gate_proj, value_proj, state_cols, step_proj], axis=1)
    spread = lax.all_to_all(normed, "seq", split_axis=1, concat_axis=0, tiled=True)
    summed = lax.psum_scatter(
        jnp.dot(spread, stacked, preferred_element_type=jnp.float32),
        "seq",
        scatter_dimension=0,
        tiled=True,
    )
    gate = summed[:, :inner_width]
    values = summed[:, inner_width : 2 * inner_width]
    states = summed[:, 2 * inner_width : 2 * inner_width + 2 * N]
    raw_step = summed[:, 2 * inner_width + 2 * N :]
    raw_mix = jnp.concatenate([values, states], axis=1).astype(jnp.bfloat16)
    tail_rows = from_behind(raw_mix[span_rows - 3 :], "seq", 1)
    extended = jnp.concatenate([tail_rows, raw_mix], axis=0)
    starts = jnp.cumsum(doc_lengths) - doc_lengths
    span_start = seq_index * span_rows
    positions = span_start - 3 + jnp.arange(span_rows + 3, dtype=jnp.int32)
    segment_ext = jnp.sum(starts[None, :] <= positions[:, None], axis=1) - 1
    segment = segment_ext[3:]
    taps = jnp.concatenate(
        [conv_value, lax.dynamic_index_in_dim(conv_state, group_index, 1, keepdims=False)], axis=1
    )
    convolved = jnp.zeros((span_rows, taps.shape[1]), jnp.float32)
    for offset in range(4):
        same_doc = segment_ext[offset : offset + span_rows] == segment
        convolved = (
            convolved
            + jnp.where(
                same_doc[:, None], extended[offset : offset + span_rows].astype(jnp.float32), 0.0
            )
            * taps[offset]
        )
    rounded = lax.optimization_barrier(jax.nn.silu(convolved).astype(jnp.bfloat16))
    activated = rounded.astype(jnp.float32)
    inputs = activated[:, :inner_width].reshape(span_rows, head_count, HEAD_DIM)
    in_map = activated[:, inner_width : inner_width + N]
    out_map = activated[:, inner_width + N :]
    in_half = rounded[:, inner_width : inner_width + N]
    out_half = rounded[:, inner_width + N :]
    step_size = jax.nn.softplus(raw_step + step_bias)
    log_decay = -decay_rate * step_size
    cumulative = jnp.cumsum(log_decay, axis=0)
    order = jnp.arange(span_rows)
    causal = (segment[:, None] == segment[None, :]) & (order[:, None] >= order[None, :])
    gaps = cumulative.T[:, :, None] - cumulative.T[:, None, :]
    decay = jnp.exp(jnp.where(causal[None], gaps, -jnp.inf))
    scores = jnp.dot(out_half, in_half.T, preferred_element_type=jnp.float32)
    mixing = decay * scores[None] * step_size.T[:, None, :]
    intra = jnp.einsum("hts,shp->thp", mixing, inputs, precision=PRECISE)
    last_segment = segment[span_rows - 1]
    prior_segment = segment_ext[2]
    in_last = segment == last_segment
    to_end = (
        jnp.where(in_last[:, None], jnp.exp(cumulative[span_rows - 1][None, :] - cumulative), 0.0)
        * step_size
    )
    local_state = jnp.einsum("sh,shp,sn->hpn", to_end, inputs, in_map, precision=PRECISE)
    passing = jnp.where(last_segment == prior_segment, jnp.exp(cumulative[span_rows - 1]), 0.0)
    empty = jnp.zeros_like(local_state)

    def relay(turn, incoming):
        return from_behind(
            (passing[:, None, None] * incoming + local_state).astype(jnp.bfloat16), "seq", 1
        ).astype(jnp.float32)

    incoming = lax.fori_loop(0, lax.axis_size("seq") - 1, relay, empty)
    carried = jnp.where((segment == prior_segment)[:, None], jnp.exp(cumulative), 0.0)
    from_state = (
        jnp.einsum("tn,hpn->thp", out_map, incoming, precision=PRECISE) * carried[:, :, None]
    )
    outputs = intra + from_state + skip_gain[None, :, None] * inputs
    gated = outputs.reshape(span_rows, inner_width) * jax.nn.silu(gate)
    squares = jnp.sum(gated * gated, axis=1)
    for bit in range(group_devices.bit_length() - 1):
        squares = squares + partner(squares, "fsdp", bit)
    scaled = (
        gated * lax.rsqrt(squares[:, None] / (H * HEAD_DIM // G) + EPSILON) * mix_gain
    ).astype(jnp.bfloat16)
    terms = jnp.dot(
        scaled,
        lax.all_gather(out_proj, "seq", axis=1, tiled=True),
        preferred_element_type=jnp.float32,
    )
    mixed = lax.psum_scatter(
        terms.astype(jnp.bfloat16), "fsdp", scatter_dimension=1, tiled=True
    ).astype(jnp.float32)
    return (tokens.astype(jnp.float32) + mixed).astype(jnp.bfloat16)


VMEM_BYTES = 20 << 20
SCAN_BYTES = 56 << 20
FIRST_BYTES = 56 << 20


def swap_cores(value):
    count = lax.axis_size("seq")
    return lax.ppermute(value, "seq", [(place, place ^ 1) for place in range(count)])


def next_chip(value, away=1):
    count = lax.axis_size("seq")
    route = [(place, (place + 2 * away) % count) for place in range(count)]
    return lax.ppermute(value, "seq", route)


def flip_fsdp(value, bits):
    count = lax.axis_size("fsdp")
    return lax.ppermute(value, "fsdp", [(place, place ^ bits) for place in range(count)])


def share_partials(pieces, projections, plan, small, thin_places, where, chips, width, grant):
    depth, count = pieces[0].shape[1], pieces[0].shape[0]
    rows = count // (2 * chips)
    number = len(pieces)
    thin_start = len(plan) * count
    thins = len(thin_places)
    thin_inputs = [small] if thins else []
    maps_width = small.shape[1] - 128
    total_rows = thin_start + thins * (rows + rows // 2)

    def body(where, *refs):
        row_refs, refs = refs[:number], refs[number:]
        weight_refs, refs = refs[: len(projections)], refs[len(projections) :]
        lent_ref, kept_ref, thin = refs[-3:]
        index, core = pl.program_id(0), where[1]
        chip = lax.rem(where[0] + chips - index, chips)
        first = core == 0

        if thins:

            @pl.when(index == 0)
            def _():
                for place, piece in enumerate(thin_places):
                    thin[place * count : (place + 1) * count] = jnp.dot(
                        row_refs[piece][...], refs[0][...], preferred_element_type=jnp.float32
                    ).astype(jnp.bfloat16)

            for out_ref, own in ((lent_ref, 1 - core), (kept_ref, core)):
                for place in range(thins):
                    at = place * count + (own * chips + chip) * rows
                    to = thin_start + place * rows
                    out_ref[0, to : to + rows] = thin[
                        pl.ds(pl.multiple_of(at, rows), rows), :maps_width
                    ]
                    to = thin_start + thins * rows + place * rows // 2
                    halves = [
                        thin[
                            pl.ds(pl.multiple_of(at + part * rows // 2, rows // 2), rows // 2),
                            maps_width:,
                        ]
                        for part in range(2)
                    ]
                    out_ref[0, to : to + rows // 2] = jnp.concatenate(halves, axis=1)

        for place, (which, piece) in enumerate(plan):
            both = jnp.dot(
                row_refs[piece][...], weight_refs[which][...], preferred_element_type=jnp.float32
            ).astype(jnp.bfloat16)
            at = slice(place * count, (place + 1) * count)
            kept_ref[0, at] = jnp.where(first, both[:, :width], both[:, width:])
            lent_ref[0, at] = jnp.where(first, both[:, width:], both[:, :width])

    out = jax.ShapeDtypeStruct((chips, total_rows, width), jnp.bfloat16)
    return pl.pallas_call(
        body,
        out_shape=[out, out],
        grid_spec=pltpu.PrefetchScalarGridSpec(
            num_scalar_prefetch=1,
            grid=(chips,),
            in_specs=[pl.BlockSpec((count, depth), lambda i, where: (0, 0)) for _ in pieces]
            + [
                pl.BlockSpec(
                    (depth, 2 * width), lambda i, where: (0, lax.rem(where[0] + chips - i, chips))
                )
                for _ in projections
            ]
            + [pl.BlockSpec(value.shape, lambda i, where: (0, 0)) for value in thin_inputs],
            out_specs=[pl.BlockSpec((1, total_rows, width), lambda i, where: (i, 0, 0))] * 2,
            scratch_shapes=[pltpu.VMEM((max(1, thins) * count, maps_width + 128), jnp.bfloat16)],
        ),
        compiler_params=pltpu.CompilerParams(vmem_limit_bytes=grant),
        name="share_partials",
    )(where, *pieces, *projections, *thin_inputs)


def add_up(*terms):
    total = terms[0].astype(jnp.float32)
    for term in terms[1:]:
        total = total + term.astype(jnp.float32)
    return total


def ring_reduce(kept, lent):
    got = swap_cores(lent)
    chips = kept.shape[0]
    passed = []
    for step in range(1, chips):
        sent = add_up(kept[step], got[step], *passed).astype(jnp.bfloat16)
        passed = [next_chip(sent)]
    return kept, got, passed[0]


def scan_heads(order, trios, groups, thin_groups, thin, thin_swapped, starts, taps, state_taps, bias, rate, skip, sizes):
    stretches, rows, quarters, width = sizes
    span = rows * quarters
    tokens = stretches * span
    count = stretches * rows
    half = rows // 2
    chips = stretches // 2
    heads = width // HEAD_DIM
    flat = [value for trio in trios for value in trio]
    number = len(flat)

    def body(order, starts_ref, *refs):
        trio_refs, refs = refs[:number], refs[number:]
        thin_ref, swapped_ref, taps_ref, state_taps_ref, bias_ref = refs[:5]
        rate_ref, skip_ref, out_ref, values, maps, steps, state, ages = refs[5:]
        token = lax.broadcasted_iota(jnp.int32, (stretches, span), 0) * span
        token = token + lax.broadcasted_iota(jnp.int32, (stretches, span), 1)
        age_rows = jnp.full((stretches, span), tokens, jnp.int32)
        for document in range(starts.shape[0]):
            since = token - starts_ref[document]
            age_rows = jnp.where(since >= 0, jnp.minimum(age_rows, since), age_rows)
        ages[...] = age_rows.astype(jnp.float32)
        first_head, chip, core = (order[quarters + place] for place in range(3))
        values[:8] = jnp.zeros((8, width), jnp.float32)
        maps[:8] = jnp.zeros((8, 2 * N), jnp.float32)

        def place_rows(stretch, carry):
            for group, members in enumerate(groups):
                kept, got, last = trio_refs[3 * group : 3 * group + 3]
                for place, k in enumerate(members):
                    at = pl.multiple_of(place * count + stretch * rows, rows)
                    to = pl.multiple_of(stretch * span + order[k] * rows, rows)
                    total = (
                        kept[0, pl.ds(at, rows), :].astype(jnp.float32)
                        + got[0, pl.ds(at, rows), :].astype(jnp.float32)
                        + last[pl.ds(at, rows), :].astype(jnp.float32)
                    )
                    values[pl.ds(to + 8, rows), :] = total.astype(jnp.bfloat16).astype(
                        jnp.float32
                    )
            return carry

        lax.fori_loop(0, stretches, place_rows, 0, unroll=2)
        for source, own_core in ((thin_ref, core), (swapped_ref, 1 - core)):
            for away in range(chips):
                stretch = own_core * chips + lax.rem(chip + chips - away, chips)
                base = 0
                for members in thin_groups:
                    for place, k in enumerate(members):
                        to = pl.multiple_of(stretch * span + order[k] * rows, rows)
                        at = base + place * rows
                        maps[pl.ds(to + 8, rows), :] = source[away, at : at + rows].astype(
                            jnp.float32
                        )
                        at = base + len(members) * rows + place * half
                        for part in range(2):
                            steps[pl.ds(pl.multiple_of(to + part * half, half), half), :] = source[
                                away, at : at + half, part * 128 : (part + 1) * 128
                            ].astype(jnp.float32)
                    base += len(members) * (rows + half)
        state[...] = jnp.zeros_like(state)
        row = lax.broadcasted_iota(jnp.int32, (span, span), 0)
        gap = row - lax.broadcasted_iota(jnp.int32, (span, span), 1)
        lower = jnp.where(gap >= 0, 1.0, 0.0)
        here = lax.broadcasted_iota(jnp.int32, (span, 1), 0)
        head_of = lax.broadcasted_iota(jnp.int32, (1, width), 1) // HEAD_DIM

        def by_head(columns):
            wide = jnp.broadcast_to(columns[:, 0:1], (columns.shape[0], width))
            for head in range(1, heads):
                wide = jnp.where(head_of == head, columns[:, head : head + 1], wide)
            return wide

        def convolve(source, gains, start, age):
            block = source[pl.ds(start, span + 8), :]
            total = block[8:] * gains[3:4]
            for lag in range(1, 4):
                total = total + jnp.where(age >= lag, block[8 - lag : 8 - lag + span], 0.0) * gains[
                    3 - lag : 4 - lag
                ]
            return (total * jax.nn.sigmoid(total)).astype(jnp.bfloat16)

        def chunk(index, carry):
            start = pl.multiple_of(index * span, span)
            age = jnp.broadcast_to(ages[pl.ds(index, 1), :], (span, span)).T.astype(jnp.int32)
            age = age[:, :1]
            last_age = age[span - 1 :]
            inputs = convolve(values, taps_ref[...], start, age)
            both = convolve(maps, state_taps_ref[...], start, age)
            in_map, out_map = both[:, :N], both[:, N:]
            raw = pltpu.roll(steps[pl.ds(start, span), :], lax.rem(128 - first_head, 128), 1)
            raw = raw + bias_ref[...]
            size = jnp.maximum(raw, 0.0) + jnp.log1p(jnp.exp(-jnp.abs(raw)))
            total = jnp.dot(
                lower,
                -rate_ref[...] * size,
                precision=PRECISE,
                preferred_element_type=jnp.float32,
            )
            total_rows, size_rows = total.T, size.T
            scores = lax.dot_general(
                out_map, in_map, (((1,), (1,)), ((), ())), preferred_element_type=jnp.float32
            )
            near = (gap >= 0) & (gap <= age)
            history = jnp.zeros((span, width), jnp.float32)
            for head in range(heads):
                decay = jnp.exp(
                    jnp.where(
                        near, total[:, head : head + 1] - total_rows[head : head + 1], -jnp.inf
                    )
                )
                mixing = (decay * scores * size_rows[head : head + 1]).astype(jnp.bfloat16)
                part = jnp.dot(mixing, inputs, preferred_element_type=jnp.float32)
                history = jnp.where(head_of == head, part, history)
            old = state[...]
            carried = by_head(jnp.where(age > here, jnp.exp(total), 0.0))
            history = history + carried * jnp.dot(
                out_map, old.astype(jnp.bfloat16), preferred_element_type=jnp.float32
            )
            wide = inputs.astype(jnp.float32)
            out_ref[pl.ds(start, span), :] = history + skip_ref[...] * wide
            end = total[span - 1 :]
            to_end = by_head(
                jnp.where(span - 1 - here <= last_age, jnp.exp(end - total), 0.0) * size
            )
            keep = by_head(jnp.where(last_age >= span, jnp.exp(end), 0.0))
            state[...] = keep * old + lax.dot_general(
                in_map,
                (wide * to_end).astype(jnp.bfloat16),
                (((0,), (0,)), ((), ())),
                preferred_element_type=jnp.float32,
            )
            return carry

        lax.fori_loop(0, stretches, chunk, 0, unroll=4)

    whole = lambda value: pl.BlockSpec(value.shape, lambda i, order, starts: (0,) * value.ndim)
    trio_specs = [
        pl.BlockSpec((1,) + value.shape[1:], lambda i, order, starts: (0, 0, 0))
        if value.ndim == 3
        else whole(value)
        for value in flat
    ]
    rest = (thin, thin_swapped, taps, state_taps, bias, rate, skip)
    return pl.pallas_call(
        body,
        out_shape=jax.ShapeDtypeStruct((tokens, width), jnp.float32),
        grid_spec=pltpu.PrefetchScalarGridSpec(
            num_scalar_prefetch=2,
            grid=(1,),
            in_specs=trio_specs + [whole(value) for value in rest],
            out_specs=pl.BlockSpec((tokens, width), lambda i, order, starts: (0, 0)),
            scratch_shapes=[
                pltpu.VMEM((tokens + 8, width), jnp.float32),
                pltpu.VMEM((tokens + 8, 2 * N), jnp.float32),
                pltpu.VMEM((tokens, 128), jnp.float32),
                pltpu.VMEM((N, width), jnp.float32),
                pltpu.VMEM((stretches, span), jnp.float32),
            ],
        ),
        compiler_params=pltpu.CompilerParams(vmem_limit_bytes=SCAN_BYTES),
        name="scan_heads",
    )(order, starts, *flat, *rest)


def gate_outputs(order, outputs, trios, groups, offsets, sizes):
    stretches, rows, quarters, width = sizes
    count, half, chips = stretches * rows, rows // 2, stretches // 2
    flat = [value for trio in trios for value in trio]
    number = len(flat)

    def body(order, *refs):
        trio_refs, outputs_ref, parts = refs[:number], refs[number], refs[number + 1 :]
        core = order[quarters + 2]

        def one_chip(chip, carry):
            for role, stretch in enumerate((2 * chip + core, 2 * chip + 1 - core)):
                for group, members in enumerate(groups):
                    kept, got, last = trio_refs[3 * group : 3 * group + 3]
                    for place, k in enumerate(members):
                        at = offsets[group] + place * count + stretch * rows
                        at = pl.ds(pl.multiple_of(at, 16), rows)
                        gate = (
                            kept[0, at, :].astype(jnp.float32)
                            + got[0, at, :].astype(jnp.float32)
                            + last[at, :].astype(jnp.float32)
                        )
                        value = (
                            outputs_ref[stretch, order[k]] * gate * jax.nn.sigmoid(gate)
                        ).astype(jnp.bfloat16)
                        for part in range(2):
                            parts[2 * role + part][chip, order[k]] = value[
                                part * half : (part + 1) * half
                            ]
            return carry

        lax.fori_loop(0, chips, one_chip, 0, unroll=2)

    whole = lambda shape: pl.BlockSpec(shape, lambda i, order: (0,) * len(shape))
    shape = (chips, quarters, half, width)
    return pl.pallas_call(
        body,
        out_shape=[jax.ShapeDtypeStruct(shape, jnp.bfloat16)] * 4,
        grid_spec=pltpu.PrefetchScalarGridSpec(
            num_scalar_prefetch=1,
            grid=(1,),
            in_specs=[
                whole((1,) + value.shape[1:] if value.ndim == 3 else value.shape)
                for value in flat
            ]
            + [whole((stretches, quarters, rows, width))],
            out_specs=[whole(shape)] * 4,
        ),
        compiler_params=pltpu.CompilerParams(vmem_limit_bytes=SCAN_BYTES),
        name="gate_outputs",
    )(order, *flat, outputs.reshape(stretches, quarters, rows, width))


def mix_channels(order, pairs, away, so_far, gains, own_proj, other_proj, sizes, grant):
    stretches, rows, quarters, width = sizes
    half, chips = rows // 2, stretches // 2
    count = pairs[0].shape[1]
    number = len(pairs) // 2
    channels, columns = own_proj.shape
    last = so_far is not None
    so_far = list(so_far) if last else []

    def owner_of(i, order):
        chip, core = order[quarters + 1], order[quarters + 2]
        return 2 * lax.rem(chip + chips - away - i // 2, chips) + lax.rem(core + i, 2)

    def body(order, *refs):
        pair_refs, refs = refs[: len(pairs)], refs[len(pairs) :]
        gains_ref, own_ref, other_ref, refs = *refs[:3], refs[3:]
        before, refs = refs[: len(so_far)], refs[len(so_far) :]
        totals = refs[5:] if last else refs
        index = pl.program_id(0)

        @pl.when(index == 0)
        def _():
            for place, total in enumerate(totals):
                total[...] = before[place][...] if last else jnp.zeros_like(total)

        for part in range(number):
            near_ref, far_ref = pair_refs[2 * part : 2 * part + 2]
            total, squares = totals[2 * part : 2 * part + 2]
            block = jnp.where(index < 2, near_ref[0], far_ref[0]).astype(jnp.float32)
            squares[...] += jnp.broadcast_to(
                jnp.sum(block * block, axis=1, keepdims=True), squares.shape
            )
            gain = gains_ref[pl.ds(owner_of(index, order), 1), :]
            gained = (block * gain).astype(jnp.bfloat16)
            for side, weights_ref in enumerate((own_ref, other_ref)):
                total[:, side * columns : (side + 1) * columns] += jnp.dot(
                    gained, weights_ref[...], preferred_element_type=jnp.float32
                )
        if last:
            total, squares, rounded = *totals, refs[4]

            @pl.when(index == pl.num_programs(0) - 1)
            def _():
                factor = lax.rsqrt(squares[:, :1] / channels + EPSILON)
                rounded[...] = (total[...] * factor).astype(jnp.bfloat16)
                left_kept, left_sent, right_kept, right_sent = refs[:4]
                for k in range(4):
                    for away in range(chips):
                        goal = lax.rem(order[quarters + 1] + away, chips)
                        at = pl.multiple_of((goal * quarters + order[k]) * half, half)
                        value = rounded[pl.ds(at, half), :]
                        (left_sent if k % 2 else left_kept)[k // 2, away] = value[:, :columns]
                        (right_sent if k // 2 else right_kept)[k % 2, away] = value[:, columns:]

    whole = lambda shape: pl.BlockSpec(shape, lambda i, order: (0,) * len(shape))
    sums = [
        jax.ShapeDtypeStruct((count, 2 * columns), jnp.float32),
        jax.ShapeDtypeStruct((count, 128), jnp.float32),
    ] * number
    part = jax.ShapeDtypeStruct((2, chips, half, columns), jnp.bfloat16)
    outs = [part] * 4 if last else sums
    scratch = [
        pltpu.VMEM((count, 2 * columns), jnp.bfloat16),
        *(pltpu.VMEM(value.shape, value.dtype) for value in sums),
    ]
    weights_spec = pl.BlockSpec((width, columns), lambda i, order: (owner_of(i, order), 0))
    pair_specs = [
        pl.BlockSpec((1, count, width), lambda i, order: (jnp.minimum(i, 1), 0, 0)),
        pl.BlockSpec((1, count, width), lambda i, order: (jnp.maximum(i - 2, 0), 0, 0)),
    ]
    return pl.pallas_call(
        body,
        out_shape=outs,
        grid_spec=pltpu.PrefetchScalarGridSpec(
            num_scalar_prefetch=1,
            grid=(4,),
            in_specs=pair_specs * number
            + [whole(gains.shape), weights_spec, weights_spec]
            + [whole(value.shape) for value in so_far],
            out_specs=[whole(value.shape) for value in outs],
            scratch_shapes=scratch if last else [],
        ),
        compiler_params=pltpu.CompilerParams(vmem_limit_bytes=grant),
        name="mix_channels",
    )(order, *pairs, gains, own_proj, other_proj, *so_far)


def add_tokens(order, tokens, pieces, sizes):
    _, rows, quarters, _ = sizes
    half = rows // 2

    def body(order, tokens_ref, *refs):
        out_ref = refs[-1]
        columns = pieces[0].shape[2]
        core = order[quarters + 2]
        for at_core in range(2):

            @pl.when(core == at_core)
            def _():
                for part, k in ((part, k) for part in range(2) for k in range(quarters)):
                    at = pl.ds(pl.multiple_of(order[k] * rows + part * half, half), half)
                    for side in range(2):
                        start = (at_core if side == 0 else 1 - at_core) * columns
                        across = slice(start, start + columns)
                        out_ref[at, across] = (
                            tokens_ref[at, across].astype(jnp.float32)
                            + refs[k][2 * part + side].astype(jnp.float32)
                        ).astype(jnp.bfloat16)

    whole = lambda value: pl.BlockSpec(value.shape, lambda i, order: (0,) * value.ndim)
    return pl.pallas_call(
        body,
        out_shape=jax.ShapeDtypeStruct(tokens.shape, tokens.dtype),
        grid_spec=pltpu.PrefetchScalarGridSpec(
            num_scalar_prefetch=1,
            grid=(1,),
            in_specs=[whole(tokens)] + [whole(value) for value in pieces],
            out_specs=whole(tokens),
        ),
        compiler_params=pltpu.CompilerParams(vmem_limit_bytes=VMEM_BYTES),
        name="add_tokens",
    )(order, tokens, *pieces)


def by_channel(
    tokens,
    norm_gain,
    gate_proj,
    value_proj,
    step_proj,
    state_proj,
    conv_value,
    conv_state,
    step_bias,
    decay_rate,
    skip_gain,
    mix_gain,
    out_proj,
    doc_lengths,
):
    stretches = lax.axis_size("seq")
    quarters = lax.axis_size("fsdp")
    chips = stretches // 2
    span, features = tokens.shape
    rows = span // quarters
    depth, inner_width = gate_proj.shape
    width = inner_width // stretches
    head_count = step_bias.shape[0]
    heads = head_count // stretches
    total_tokens = stretches * span
    sizes = (stretches, rows, quarters, width)
    seq_index = lax.axis_index("seq")
    fsdp_index = lax.axis_index("fsdp")
    chip, core = seq_index // 2, seq_index % 2
    where = jnp.stack([chip, core])
    order = jnp.stack(
        [fsdp_index ^ k for k in range(quarters)]
        + [(seq_index * heads).astype(jnp.int32), chip, core]
    )

    state_cols = lax.dynamic_index_in_dim(state_proj, fsdp_index, 1, keepdims=False)
    small = jnp.concatenate(
        [state_cols, step_proj, jnp.zeros((depth, 128 - head_count), jnp.bfloat16)], axis=1
    )
    starts = (jnp.cumsum(doc_lengths) - doc_lengths).astype(jnp.int32)
    own_part = lambda value: lax.dynamic_slice_in_dim(value, seq_index * heads, heads, 0)
    lanes = lambda value: jnp.pad(own_part(value), (0, 128 - heads))[None, :]
    bias, rate = lanes(step_bias), lanes(decay_rate)
    skip = jnp.repeat(own_part(skip_gain), HEAD_DIM)[None, :]
    taps = lax.dynamic_slice_in_dim(conv_value, seq_index * width, width, 1)
    state_taps = lax.dynamic_index_in_dim(conv_state, fsdp_index, 1, keepdims=False)

    other_proj = swap_cores(out_proj)
    parts = lax.all_to_all(
        tokens.reshape(quarters, rows, features), "fsdp", split_axis=0, concat_axis=0, tiled=True
    )
    as_float = parts.astype(jnp.float32)
    mean_square = jnp.sum(as_float * as_float, axis=(0, 2), keepdims=True) / (
        quarters * features
    )
    normed = (
        as_float * lax.rsqrt(mean_square + EPSILON) * norm_gain.reshape(quarters, 1, features)
    ).astype(jnp.bfloat16)
    slices = (
        normed.reshape(quarters, rows, stretches // quarters, depth)
        .transpose(0, 2, 1, 3)
        .reshape(stretches, rows, depth)
    )
    own = lax.all_to_all(slices, "seq", split_axis=0, concat_axis=0, tiled=True).reshape(
        stretches * rows, depth
    )
    own, small, starts, bias, rate, skip, taps, state_taps, order, where = lax.optimization_barrier(
        (own, small, starts, bias, rate, skip, taps, state_taps, order, where)
    )

    near = [flip_fsdp(own, 1), flip_fsdp(own, 2)]
    middle = own.shape[0] // 2
    upper = flip_fsdp(near[1][:middle], 1)
    lower = flip_fsdp(near[0][middle:], 2)
    pieces = [own, *near, jnp.concatenate([upper, lower], axis=0)]

    def reduced(members, projections, plan, thin_places=(), grant=VMEM_BYTES):
        lent, kept = share_partials(
            [pieces[k] for k in members], projections, plan, small, thin_places, where,
            chips, width, grant,
        )
        return ring_reduce(kept, lent)

    count = stretches * rows
    first = reduced((0,), [value_proj, gate_proj], ((0, 0), (1, 0)), (0,), FIRST_BYTES)
    second = reduced((3, 1, 2), [value_proj], ((0, 0),), (0, 1, 2))
    third = reduced((1, 2), [value_proj], ((0, 0), (0, 1)))
    fourth = reduced((1, 2, 3), [gate_proj], ((0, 0), (0, 1), (0, 2)))
    value_groups, thin_groups = ((0,), (3,), (1, 2)), ((0,), (3, 1, 2))
    gate_groups, gate_starts = ((0,), (1, 2, 3)), (count, 0)
    thin = jnp.concatenate(
        [
            add_up(trio[0][0, start:], trio[1][0, start:], trio[2][start:]).astype(
                jnp.bfloat16
            )
            for trio, start in ((first, 2 * count), (second, count))
        ]
    )
    spread = [thin]
    for _ in range(1, chips):
        spread.append(next_chip(spread[-1]))
    thin = jnp.stack(spread)
    thin_swapped = swap_cores(thin)
    outputs = scan_heads(
        order, (first, second, third), value_groups, thin_groups, thin, thin_swapped, starts, taps, state_taps,
        bias, rate, skip, sizes,
    )
    parts = gate_outputs(order, outputs, (first, fourth), gate_groups, gate_starts, sizes)
    gains = mix_gain.reshape(stretches, width)
    sums, shares = [], []
    for part in range(2):
        flat = lambda value: value.reshape(total_tokens // 4, width)
        came = swap_cores(parts[2 + part])
        blocks = [jnp.stack([flat(parts[part]), flat(came)])]
        for _ in range(1, chips):
            blocks.append(next_chip(blocks[-1]))
        shares.append(blocks)
    so_far = mix_channels(
        order, shares[0][:2] + shares[1][:2], 0, None, gains, out_proj, other_proj, sizes,
        VMEM_BYTES,
    )
    for part in range(2):
        left_kept, left_sent, right_kept, right_sent = mix_channels(
            order, shares[part][2:], 2, so_far[2 * part : 2 * part + 2], gains, out_proj,
            other_proj, sizes, VMEM_BYTES,
        )
        left_got = flip_fsdp(left_sent, 1)
        right_got = flip_fsdp(right_sent, 2)
        left_sum = add_up(left_kept[1], left_got[1]).astype(jnp.bfloat16)
        right_sum = add_up(right_kept[1], right_got[1]).astype(jnp.bfloat16)
        left_more = flip_fsdp(left_sum, 2)
        right_more = flip_fsdp(right_sum, 1)
        sums.append((left_kept[0], left_got[0], left_more, right_kept[0], right_got[0], right_more))

    def to_chip(away):
        pick = lambda terms: add_up(*(term[away] for term in terms)).astype(jnp.bfloat16)
        return jnp.stack([pick(terms[side : side + 3]) for terms in sums for side in (0, 3)])

    arrived = [to_chip(0)]
    for away in range(1, chips):
        arrived.append(next_chip(to_chip(away), away))

    def from_chip(other):
        back = (chip + chips - other) % chips
        value = arrived[0]
        for away in range(1, chips):
            value = jnp.where(back == away, arrived[away], value)
        return value

    ended = [from_chip(fsdp_index)]
    for k in range(1, quarters):
        ended.append(flip_fsdp(from_chip(fsdp_index ^ k), k))
    return add_tokens(order, tokens, ended, sizes)


def layer(*arguments):
    stretches, quarters = lax.axis_size("seq"), lax.axis_size("fsdp")
    span, inner_width = arguments[0].shape[0], arguments[2].shape[1]
    heads = arguments[8].shape[0]
    width = inner_width // stretches
    aligned = (
        quarters == G
        and quarters == 4
        and stretches == 2 * quarters
        and width == 2 * N
        and width % HEAD_DIM == 0
        and heads <= 128
        and span % (16 * quarters) == 0
        and span % 128 == 0
    )
    return (by_channel if aligned else by_stretch)(*arguments)


def solution(mesh):
    return jax.shard_map(
        layer,
        mesh=mesh,
        in_specs=(
            P("seq", "fsdp"),
            P(),
            P("seq", "fsdp"),
            P("seq", "fsdp"),
            P("seq", "fsdp"),
            P("seq", None, None),
            P(None, "fsdp"),
            P(),
            P("fsdp"),
            P("fsdp"),
            P("fsdp"),
            P("fsdp"),
            P("fsdp", "seq"),
            P(),
        ),
        out_specs=P("seq", "fsdp"),
        check_vma=False,
    )
```
